32 devices in a mesh: gx: 8 (over y, x, core), gy: 4 (over z).
Axes of the slice: x: 2, y: 2, z: 4, core: 2. Of those that a mesh axis runs over, the one named last changes fastest.
Arguments:
- latent: bfloat16 [13824, 128], P(('gx', 'gy')), may hold values from -6 to 6
- offset: bfloat16 [2, 13824], P(None, ('gx', 'gy')), may hold values from 0 to 1
- owner: int32 [13824], P(('gx', 'gy')), may hold values from 0 to 31, as said below
- slot: int32 [13824], P(('gx', 'gy')), may hold values from -1 to 511, as said below
- cotangent: bfloat16 [64, 32, 8, 128], P('gx', 'gy'), may hold values from -6 to 6
- edge_in: bfloat16 [2, 128, 256], replicated, may hold values from -0.5 to 0.5
- edge_geo: bfloat16 [2, 3, 128], replicated, may hold values from -3.5 to 3.5
- edge_mid: bfloat16 [2, 128, 128], replicated, may hold values from -0.5 to 0.5
- edge_out: bfloat16 [2, 128, 128], replicated, may hold values from -0.25 to 0.25
- node_in: bfloat16 [2, 256, 128], replicated, may hold values from -0.375 to 0.375
- node_out: bfloat16 [2, 128, 128], replicated, may hold values from -0.5 to 0.5
- biases: bfloat16 [2, 5, 128], replicated, may hold values from -3 to 3
- ln_gain: bfloat16 [2, 128], replicated, may hold values from 0.5 to 1.5
Outputs:
- latent_out: bfloat16 [64, 32, 8, 128], P('gx', 'gy')
- latent_grad: float32 [64, 32, 8, 128], P('gx', 'gy')
- grad_edge_in: float32 [2, 128, 256], replicated
- grad_edge_geo: float32 [2, 3, 128], replicated
- grad_edge_mid: float32 [2, 128, 128], replicated
- grad_edge_out: float32 [2, 128, 128], replicated
- grad_node_in: float32 [2, 256, 128], replicated
- grad_node_out: float32 [2, 128, 128], replicated
- grad_biases: float32 [2, 5, 128], replicated
- grad_ln_gain: float32 [2, 128], replicated
The draws below stay inside these ranges and needn't reach their ends.
Inputs may be any that keep to these rules, and one draw needn't show every extreme that they name: `owner`: the 432 rows of each device name each of the nine devices at offsets -1, 0, +1 along gx and along gy (wrapping around, the device itself included) exactly 48 times. Cell (cx, cy) of a device holds slots (cx * 8 + cy) * 8 to (cx * 8 + cy) * 8 + 7. No slot of a device is named by two rows. In every draw some cell of every device receives 8 particles, and every device has 48 rows with particles for one of its neighbours.
All inputs are finite; a program needn't handle non-finite values.
Results may differ from the reference program's by a relative error of at most 0.019.
Values may be sent and summed in bfloat16 or wider, within the bound.
No kernel may reach another device: no remote copies, remote signals or barrier semaphores. Data moves between devices by JAX's collectives and lax.ppermute only.
A program may use at most 64 MiB of HBM per device.

```python
import jax
import jax.numpy as jnp
from jax import lax

L = 128
STEPS = 2
CAP = 8
CXD = 8
CYD = 8
PARTICLES = 13824
NXC = 64
NYC = 32
N_GX = 8
N_GY = 4


def rebin_plan(key):
    base_key = jax.random.fold_in(key, 11)
    key_list = jax.random.split(base_key, 4)
    device_count = N_GX * N_GY
    slot_count = CXD * CYD * CAP
    send_rows = slot_count * 3 // 32
    row_count = 9 * send_rows

    def permute_rows(one_key):
        return jax.random.permutation(one_key, row_count)

    def permute_others(one_key):
        return jax.random.permutation(one_key, slot_count - CAP)
    sender_order = jax.vmap(permute_rows)(jax.random.split(key_list[0], device_count)).astype(jnp.int32)
    bucket = sender_order // send_rows
    step_x = bucket // 3 - 1
    step_y = bucket % 3 - 1
    device_ids = jnp.arange(device_count, dtype=jnp.int32)[:, None]
    owner_ids = (device_ids // N_GY + step_x) % N_GX * N_GY + (device_ids % N_GY + step_y) % N_GY
    full_cell = jax.random.randint(key_list[1], (device_count,), 0, CXD * CYD).astype(jnp.int32)
    other_slots = jax.vmap(permute_others)(jax.random.split(key_list[2], device_count)).astype(jnp.int32)
    other_slots = other_slots + CAP * (other_slots >= full_cell[:, None] * CAP).astype(jnp.int32)
    arrival = jnp.arange(row_count, dtype=jnp.int32)[None, :]
    later = jnp.broadcast_to(jnp.clip(arrival - CAP, 0, slot_count - CAP - 1), (device_count, row_count))
    from_other = jnp.take_along_axis(other_slots, later, axis=1)
    slot_map = jnp.where(arrival < CAP, full_cell[:, None] * CAP + arrival, from_other)
    chance = jax.random.randint(key_list[3], (device_count, row_count), 0, 4)
    live = (arrival < max(send_rows, CAP)) | (chance > 0)
    owner_slot = jnp.where(live, slot_map, -1)
    slot_ids = owner_slot[owner_ids, sender_order]
    return (owner_ids.reshape(-1).astype(jnp.int32), slot_ids.reshape(-1).astype(jnp.int32))


def draw_owner(key, part):
    return rebin_plan(key)[0]


def draw_slot(key, part):
    return rebin_plan(key)[1]


def steps_of(rng, dims, pieces, least, high):
    level, own = 1.0, jax.random.fold_in(rng, 6)
    for axis_at, shards_of in pieces:
        steps = jnp.exp(jax.random.uniform(jax.random.fold_in(own, axis_at), (shards_of,), jnp.float32, least / len(pieces), high / len(pieces)))
        level = level * jnp.repeat(steps, dims[axis_at] // shards_of).reshape([-1 if axis == axis_at else 1 for axis in range(len(dims))])
    return level


def normal_values(rng, extent, width, bound, shards=(), held_as=jnp.bfloat16):
    entries = jax.random.normal(rng, extent, jnp.float32) * width
    if len(shards) > 0:
        entries = steps_of(rng, extent, shards, -0.22, 0.18) * entries
    return jnp.clip(entries, min=-bound, max=bound).astype(held_as)


def setup_inputs(seed: int = 0) -> dict:
    splits = jax.random.split(jax.random.key(seed), 14)
    latent = normal_values(splits[0], (PARTICLES, L), 1.0, 6.0, ((0, 32),))
    offset = jnp.clip(1.0 * jax.random.uniform(splits[1], (2, PARTICLES), jnp.float32) ** steps_of(splits[1], (2, PARTICLES), ((1, 32),), -0.2, 0.2), 0.0, 1.0).astype(jnp.bfloat16)
    owner = draw_owner(jax.random.fold_in(splits[13], 71), 0)
    slot = draw_slot(jax.random.fold_in(splits[13], 71), 0)
    cotangent = normal_values(splits[4], (NXC, NYC, CAP, L), 1.0, 6.0, ((0, 8), (1, 4)))
    edge_in = normal_values(splits[5], (STEPS, L, 2 * L), L ** -0.5, 0.5)
    edge_geo = normal_values(splits[6], (STEPS, 3, L), 3 ** -0.5, 3.5)
    edge_mid = normal_values(splits[7], (STEPS, L, L), L ** -0.5, 0.5)
    edge_out = normal_values(splits[8], (STEPS, L, L), (4 * L) ** -0.5, 0.25)
    node_in = normal_values(splits[9], (STEPS, 2 * L, L), (2 * L) ** -0.5, 0.375)
    node_out = normal_values(splits[10], (STEPS, L, L), L ** -0.5, 0.5)
    biases = normal_values(splits[11], (STEPS, 5, L), 0.5, 3.0)
    ln_gain = jnp.clip(1.0 + 0.1 * jax.random.normal(splits[12], (STEPS, L), jnp.float32), 0.5, 1.5).astype(jnp.bfloat16)
    return dict(latent=latent, offset=offset, owner=owner, slot=slot, cotangent=cotangent, edge_in=edge_in, edge_geo=edge_geo, edge_mid=edge_mid, edge_out=edge_out, node_in=node_in, node_out=node_out, biases=biases, ln_gain=ln_gain)


LN_EPS = 1e-05

def silu_slope(values):
    sigmoid_value = jax.nn.sigmoid(values)
    return sigmoid_value * (1.0 + values * (1.0 - sigmoid_value))

def edge_geometry(geo_own, geo_near):
    cap_size = geo_own.shape[2]
    near_count = geo_near.shape[2]
    near_index = jnp.arange(near_count)
    near_block = near_index // cap_size
    shift_x = (near_block // 3 - 1).astype(jnp.float32)
    shift_y = (near_block % 3 - 1).astype(jnp.float32)
    own_index = jnp.arange(cap_size)
    not_self = (near_index[None, :] != 4 * cap_size + own_index[:, None]).astype(jnp.float32)
    delta_x = shift_x + geo_near[:, 0, None, :] - geo_own[:, 0, :, None]
    delta_y = shift_y + geo_near[:, 1, None, :] - geo_own[:, 1, :, None]
    radius_sq = delta_x * delta_x + delta_y * delta_y
    reach = jnp.maximum(1.0 - radius_sq, 0.0)
    edge_weight = geo_own[:, 2, :, None] * geo_near[:, 2, None, :] * reach * reach * not_self
    return (delta_x, delta_y, radius_sq, edge_weight)

def edge_hidden(own_part, far_near, delta_x, delta_y, radius_sq, geo_weight, mid_weight, mid_bias):
    latent_width = own_part.shape[-1]
    geo_float = geo_weight.astype(jnp.float32)
    pre_one = own_part[:, :, None, :] + far_near[:, None, :, :].astype(jnp.float32)
    pre_one = pre_one + delta_x[..., None] * geo_float[0] + delta_y[..., None] * geo_float[1]
    pre_one = pre_one + radius_sq[..., None] * geo_float[2]
    hidden_one = jax.nn.silu(pre_one).astype(jnp.bfloat16)
    pre_two = jnp.dot(hidden_one.reshape(-1, latent_width), mid_weight, preferred_element_type=jnp.float32)
    pre_two = pre_two.reshape(pre_one.shape) + mid_bias.astype(jnp.float32)
    return (pre_one, hidden_one, pre_two)

def edge_forward(own_part, far_near, geo_own, geo_near, geo_weight, mid_weight, mid_bias):
    delta_x, delta_y, radius_sq, edge_weight = edge_geometry(geo_own, geo_near)
    pre_one, hidden_one, pre_two = edge_hidden(own_part, far_near, delta_x, delta_y, radius_sq, geo_weight, mid_weight, mid_bias)
    edge_sums = jnp.einsum('ncj,ncjh->nch', edge_weight, jax.nn.silu(pre_two))
    return (edge_sums, lax.optimization_barrier(jnp.sum(edge_weight, axis=2)))

def edge_backward(d_sums, own_part, far_near, geo_own, geo_near, geo_weight, mid_weight, mid_bias):
    latent_width = own_part.shape[-1]
    delta_x, delta_y, radius_sq, edge_weight = edge_geometry(geo_own, geo_near)
    pre_one, hidden_one, pre_two = edge_hidden(own_part, far_near, delta_x, delta_y, radius_sq, geo_weight, mid_weight, mid_bias)
    d_pre_two = edge_weight[..., None] * d_sums[:, :, None, :] * silu_slope(pre_two)
    d_two_low = d_pre_two.astype(jnp.bfloat16).reshape(-1, latent_width)
    grad_mid = jnp.dot(hidden_one.reshape(-1, latent_width).T, d_two_low, preferred_element_type=jnp.float32)
    grad_bias = lax.optimization_barrier(jnp.sum(d_pre_two, axis=(0, 1, 2)))
    d_pre_one = jnp.dot(d_two_low, mid_weight.T, preferred_element_type=jnp.float32).reshape(pre_one.shape)
    d_pre_one = d_pre_one * silu_slope(pre_one)
    grad_geo = jnp.stack([jnp.einsum('ncj,ncjh->h', delta_x, d_pre_one), jnp.einsum('ncj,ncjh->h', delta_y, d_pre_one), jnp.einsum('ncj,ncjh->h', radius_sq, d_pre_one)])
    return (lax.optimization_barrier(jnp.sum(d_pre_one, axis=2)), lax.optimization_barrier(jnp.sum(d_pre_one, axis=1)), grad_geo, grad_mid, grad_bias)

def node_forward(latent_flat, occupied, edge_sums, weight_sum, out_weight, first_weight, second_weight, bias_rows, gain_row):
    latent_width = latent_flat.shape[1]
    bias_float = bias_rows.astype(jnp.float32)
    sums_low = edge_sums.astype(jnp.bfloat16)
    message = jnp.dot(sums_low, out_weight, preferred_element_type=jnp.float32) + weight_sum[:, None] * bias_float[1]
    message_low = message.astype(jnp.bfloat16)
    first_pre = jnp.dot(latent_flat, first_weight[:latent_width], preferred_element_type=jnp.float32)
    first_pre = first_pre + jnp.dot(message_low, first_weight[latent_width:], preferred_element_type=jnp.float32) + bias_float[2]
    first_low = jax.nn.silu(first_pre).astype(jnp.bfloat16)
    second_pre = jnp.dot(first_low, second_weight, preferred_element_type=jnp.float32) + bias_float[3]
    centred = second_pre - lax.optimization_barrier(jnp.mean(second_pre, axis=1, keepdims=True))
    inv_root = lax.rsqrt(lax.optimization_barrier(jnp.mean(centred * centred, axis=1, keepdims=True)) + LN_EPS)
    normed = centred * inv_root
    update = normed * gain_row.astype(jnp.float32) + bias_float[4]
    new_latent = (latent_flat.astype(jnp.float32) + occupied[:, None] * update).astype(jnp.bfloat16)
    return (new_latent, (sums_low, message_low, first_pre, first_low, normed, inv_root))

def node_backward(d_new, latent_flat, occupied, weight_sum, saved, out_weight, first_weight, second_weight, gain_row):
    latent_width = latent_flat.shape[1]
    sums_low, message_low, first_pre, first_low, normed, inv_root = saved
    d_update = occupied[:, None] * d_new
    grad_gain = lax.optimization_barrier(jnp.sum(d_update * normed, axis=0))
    grad_shift = lax.optimization_barrier(jnp.sum(d_update, axis=0))
    d_normed = d_update * gain_row.astype(jnp.float32)
    d_second = inv_root * (d_normed - lax.optimization_barrier(jnp.mean(d_normed, axis=1, keepdims=True)) - normed * lax.optimization_barrier(jnp.mean(d_normed * normed, axis=1, keepdims=True)))
    d_second_low = d_second.astype(jnp.bfloat16)
    grad_second = jnp.dot(first_low.T, d_second_low, preferred_element_type=jnp.float32)
    grad_second_bias = lax.optimization_barrier(jnp.sum(d_second, axis=0))
    d_first = jnp.dot(d_second_low, second_weight.T, preferred_element_type=jnp.float32) * silu_slope(first_pre)
    d_first_low = d_first.astype(jnp.bfloat16)
    grad_first = jnp.concatenate([jnp.dot(latent_flat.T, d_first_low, preferred_element_type=jnp.float32), jnp.dot(message_low.T, d_first_low, preferred_element_type=jnp.float32)], axis=0)
    grad_first_bias = lax.optimization_barrier(jnp.sum(d_first, axis=0))
    d_latent = jnp.dot(d_first_low, first_weight[:latent_width].T, preferred_element_type=jnp.float32)
    d_message = jnp.dot(d_first_low, first_weight[latent_width:].T, preferred_element_type=jnp.float32)
    d_message_low = d_message.astype(jnp.bfloat16)
    grad_out = jnp.dot(sums_low.T, d_message_low, preferred_element_type=jnp.float32)
    grad_out_bias = lax.optimization_barrier(jnp.sum(weight_sum[:, None] * d_message, axis=0))
    d_sums = jnp.dot(d_message_low, out_weight.T, preferred_element_type=jnp.float32)
    return (d_sums, d_latent, (grad_out, grad_first, grad_second, grad_out_bias, grad_first_bias, grad_second_bias, grad_shift, grad_gain))

def reference(latent, offset, owner, slot, cotangent, edge_in, edge_geo, edge_mid, edge_out, node_in, node_out, biases, ln_gain):
    device_count = N_GX * N_GY
    slot_count = CXD * CYD * CAP
    total_slots = device_count * slot_count
    target = jnp.where(slot >= 0, owner * slot_count + slot, total_slots).astype(jnp.int32)
    placed = jnp.zeros((total_slots, L), jnp.bfloat16).at[target].set(latent, mode='drop')
    place_x = jnp.zeros((total_slots,), jnp.float32).at[target].set(offset[0].astype(jnp.float32), mode='drop')
    place_y = jnp.zeros((total_slots,), jnp.float32).at[target].set(offset[1].astype(jnp.float32), mode='drop')
    occupied = jnp.zeros((total_slots,), jnp.float32).at[target].set(1.0, mode='drop')

    def to_grid(values):
        trailing = values.shape[1:]
        shaped = values.reshape((N_GX, N_GY, CXD, CYD, CAP) + trailing)
        order = (0, 2, 1, 3) + tuple(range(4, 5 + len(trailing)))
        return shaped.transpose(order).reshape((NXC, NYC, CAP) + trailing)
    latent_now = to_grid(placed)
    occupied_grid = to_grid(occupied)
    occupied_flat = occupied_grid.reshape(-1)
    geo_cells = jnp.stack([to_grid(place_x), to_grid(place_y), occupied_grid], axis=2)
    move_list = [(shift_a, shift_b) for shift_a in (-1, 0, 1) for shift_b in (-1, 0, 1)]
    geo_near = jnp.stack([jnp.roll(geo_cells, (-shift_a, -shift_b), (0, 1)) for shift_a, shift_b in move_list], axis=3)
    geo_near = geo_near.reshape(NXC, NYC, 3, 9 * CAP)
    saved_steps = []
    for step_index in range(STEPS):
        flat_rows = latent_now.reshape(-1, L)
        both_parts = jnp.dot(flat_rows, edge_in[step_index], preferred_element_type=jnp.float32)
        own_part = both_parts[:, :L].reshape(NXC, NYC, CAP, L)
        far_part = both_parts[:, L:].astype(jnp.bfloat16).reshape(NXC, NYC, CAP, L)
        far_near = jnp.stack([jnp.roll(far_part, (-shift_a, -shift_b), (0, 1)) for shift_a, shift_b in move_list], axis=2)
        far_near = far_near.reshape(NXC, NYC, 9 * CAP, L)

        def row_forward(row_items):
            own_row, near_row, geo_row, geo_near_row = row_items
            return edge_forward(own_row, near_row, geo_row, geo_near_row, edge_geo[step_index], edge_mid[step_index], biases[step_index, 0])
        edge_sums, weight_sum = lax.map(row_forward, (own_part, far_near, geo_cells, geo_near))
        weight_flat = weight_sum.reshape(-1)
        new_latent, saved = node_forward(flat_rows, occupied_flat, edge_sums.reshape(-1, L), weight_flat, edge_out[step_index], node_in[step_index], node_out[step_index], biases[step_index], ln_gain[step_index])
        saved_steps.append((flat_rows, own_part, far_near, weight_flat, saved))
        latent_now = new_latent.reshape(NXC, NYC, CAP, L)
    grad_now = cotangent.astype(jnp.float32).reshape(-1, L)
    grad_steps = [None] * STEPS
    for step_index in reversed(range(STEPS)):
        flat_rows, own_part, far_near, weight_flat, saved = saved_steps[step_index]
        d_sums, d_latent, node_grads = node_backward(grad_now, flat_rows, occupied_flat, weight_flat, saved, edge_out[step_index], node_in[step_index], node_out[step_index], ln_gain[step_index])

        def row_backward(row_items):
            d_row, own_row, near_row, geo_row, geo_near_row = row_items
            return edge_backward(d_row, own_row, near_row, geo_row, geo_near_row, edge_geo[step_index], edge_mid[step_index], biases[step_index, 0])
        d_own, d_near, grad_geo, grad_mid, grad_mid_bias = lax.map(row_backward, (d_sums.reshape(NXC, NYC, CAP, L), own_part, far_near, geo_cells, geo_near))
        d_near = d_near.reshape(NXC, NYC, 9, CAP, L)
        d_far = jnp.zeros((NXC, NYC, CAP, L), jnp.float32)
        for move_index, (shift_a, shift_b) in enumerate(move_list):
            d_far = d_far + jnp.roll(d_near[:, :, move_index], (shift_a, shift_b), (0, 1))
        d_both = jnp.concatenate([d_own.reshape(-1, L), d_far.reshape(-1, L)], axis=1).astype(jnp.bfloat16)
        grad_in = jnp.dot(flat_rows.T, d_both, preferred_element_type=jnp.float32)
        grad_now = grad_now + d_latent + jnp.dot(d_both, edge_in[step_index].T, preferred_element_type=jnp.float32)
        grad_out, grad_first, grad_second, grad_out_bias, grad_first_bias, grad_second_bias, grad_shift, grad_gain = node_grads
        bias_grads = jnp.stack([lax.optimization_barrier(jnp.sum(grad_mid_bias, axis=0)), grad_out_bias, grad_first_bias, grad_second_bias, grad_shift])
        grad_steps[step_index] = (grad_in, lax.optimization_barrier(jnp.sum(grad_geo, axis=0)), lax.optimization_barrier(jnp.sum(grad_mid, axis=0)), grad_out, grad_first, grad_second, bias_grads, grad_gain)
    grad_scale = float(total_slots) ** (-0.5)
    stacked = [jnp.stack([grad_steps[step_index][member] for step_index in range(STEPS)]) * grad_scale for member in range(8)]
    latent_grad = (grad_now * occupied_flat[:, None]).reshape(NXC, NYC, CAP, L)
    return (latent_now, latent_grad, stacked[0], stacked[1], stacked[2], stacked[3], stacked[4], stacked[5], stacked[6], stacked[7])
```

```python
import functools

import jax
import jax.numpy as jnp
from jax import lax
from jax.experimental import pallas as pl
from jax.experimental.pallas import tpu as pltpu
from jax.sharding import PartitionSpec as P

STEPS = 2
LN_EPS = 1e-05
F32 = jnp.float32
BF = jnp.bfloat16
L = 128
CAP = 8
NEAR = 9 * CAP
EDGES = CAP * NEAR
GROWS = 1024


def dot(a, b):
    return jnp.dot(a, b, preferred_element_type=F32)


def dot_tn(a, b):
    return lax.dot_general(a, b, (((0,), (0,)), ((), ())), preferred_element_type=F32)


def dot_nt(a, b):
    return lax.dot_general(a, b, (((1,), (1,)), ((), ())), preferred_element_type=F32)


def iota(shape, dim):
    return lax.broadcasted_iota(jnp.int32, shape, dim)


def mask(cond):
    return jnp.where(cond, 1.0, 0.0).astype(F32)


def slope_of(half, tanh_half):
    sig = 0.5 + 0.5 * tanh_half
    act = half + half * tanh_half
    return sig + act * (1.0 - sig)


def sort_kernel(latent_ref, bucket_ref, meta_ref, out_ref):
    rows = latent_ref.shape[0]
    send = rows // 9
    bucket = bucket_ref[...]
    hot = mask(iota((16, rows), 0) == bucket)
    upper = mask(iota((rows, rows), 0) <= iota((rows, rows), 1)).astype(BF)
    count = dot(hot.astype(BF), upper)
    rank = jnp.sum(hot * (count - 1.0), axis=0, keepdims=True)
    target = bucket.astype(F32) * float(send) + rank
    perm = mask(iota((rows, rows), 0).astype(F32) == target).astype(BF)
    out_ref[:, :L] = dot(perm, latent_ref[...]).astype(BF)
    meta = jnp.concatenate([meta_ref[...], jnp.zeros((L - 8, rows), F32)], axis=0).astype(BF)
    out_ref[:, L:] = dot_nt(perm, meta).astype(BF)


def place_kernel(rows_ref, edge_in_ref, latent_ref, own_ref, pay_ref):
    rows = rows_ref.shape[0]
    slots = latent_ref.shape[0]
    pick_lane = iota((8, L), 1)
    pick = jnp.where(pick_lane == 3, 16.0, jnp.where(pick_lane == 4, 1.0, 0.0)).astype(BF)
    mark = dot_nt(pick, rows_ref[:, L:])[0:1]
    hot = mask((iota((slots, rows), 0) + 1).astype(F32) == mark).astype(BF)
    placed = dot(hot, rows_ref[...]).astype(BF)
    latent = placed[:, :L]
    latent_ref[...] = latent
    both = dot(latent, edge_in_ref[...])
    own_ref[...] = both[:, :L]
    pay_ref[:, :L] = both[:, L:].astype(BF)
    pay_ref[:, L:] = placed[:, L:]


def fill_geometry(geo, width, lhs_ref, weight_ref, weight_t_ref, radius_t_ref, hot_t_ref):
    halo_rows = geo.shape[0]
    rows = dot_nt(mask(iota((8, L), 0) == iota((8, L), 1)).astype(BF), geo)
    cell = iota((halo_rows, L), 1) * CAP
    row = iota((halo_rows, L), 0)
    cell_hot = mask((row >= cell) & (row < cell + CAP)).astype(BF)
    slot_hot = mask((iota((8, halo_rows), 1) & (CAP - 1)) == iota((8, halo_rows), 0))
    px, py, occ = (dot((slot_hot * rows[k : k + 1]).astype(BF), cell_hot) for k in range(3))
    near = ([], [], [])
    for a in (-1, 0, 1):
        for b in (-1, 0, 1):
            shift = (-(width * a + b)) % L
            for piece, value, base in zip(near, (px, py, occ), (a, b, 0)):
                moved = value if shift == 0 else pltpu.roll(value, shift, 1)
                piece.append(moved + float(base))
    near_x, near_y, near_occ = (jnp.concatenate(piece, axis=0) for piece in near)
    radius, weight, hots = [], [], []
    lane = iota((NEAR, L), 1)
    sub = iota((NEAR, L), 0)
    for i in range(CAP):
        dx = near_x - px[i : i + 1]
        dy = near_y - py[i : i + 1]
        r2 = dx * dx + dy * dy
        reach = jnp.maximum(1.0 - r2, 0.0)
        w = occ[i : i + 1] * near_occ * reach * reach
        radius.append(r2)
        weight.append(jnp.where(sub == 4 * CAP + i, 0.0, w))
        hots.append(mask((sub == lane) | (lane == NEAR + i) | (lane == NEAR + CAP + i)))
    radius = jnp.concatenate(radius, axis=0)
    weight = jnp.concatenate(weight, axis=0)
    hots = jnp.concatenate(hots, axis=0)
    lhs_ref[:, :L] = hots.astype(BF)
    lhs_ref[:, L:] = radius.astype(BF)
    weight_ref[...] = weight.astype(BF)
    weight_t_ref[...] = weight.T
    radius_t_ref[...] = radius.T
    hot_t_ref[...] = hots.T[:80].astype(BF)


def column(value, k):
    return value[:, k : k + 1].astype(F32)


def fill_pre(far, geo_halo, own, geo_own, edge_geo, far_ref, near_ref):
    g0 = 0.5 * edge_geo[0:1].astype(F32)
    g1 = 0.5 * edge_geo[1:2].astype(F32)
    far_ref[...] = 0.5 * far.astype(F32) + column(geo_halo, 0) * g0 + column(geo_halo, 1) * g1
    near_ref[...] = 0.5 * own - column(geo_own, 0) * g0 - column(geo_own, 1) * g1


def shift_rows(edge_geo):
    g0 = 0.5 * edge_geo[0:1].astype(F32)
    g1 = 0.5 * edge_geo[1:2].astype(F32)
    side = iota((3 * CAP, L), 0) // CAP - 1
    return [float(a) * g0 + side.astype(F32) * g1 for a in (-1, 0, 1)]


def twice(row):
    return jnp.concatenate([row, row], axis=1)


def block_diag(w):
    zero = jnp.zeros_like(w)
    return jnp.concatenate(
        [jnp.concatenate([w, zero], axis=1), jnp.concatenate([zero, w], axis=1)], axis=0
    )


def pair_place(pair, cells_y):
    half = cells_y // 2
    x = pair // half
    y = (pair - x * half) * 2
    return x, y


def pair_rhs(pair, width, far_ref, near_ref, shifts, g2):
    x, y = pair_place(pair, width - 2)
    tops = []
    for k in range(2):
        pieces = []
        for a in range(3):
            start = pl.multiple_of(((x + a) * width + y + k) * CAP, CAP)
            pieces.append(far_ref[pl.ds(start, 3 * CAP), :] + shifts[a])
        mine = near_ref[pl.ds(pl.multiple_of((pair * 2 + k) * CAP, CAP), CAP), :]
        pieces.append(mine)
        pieces.append(mine - mine.astype(BF).astype(F32))
        pieces.append(jnp.zeros((L - NEAR - 2 * CAP, L), F32))
        tops.append(jnp.concatenate(pieces, axis=0))
    top = jnp.concatenate(tops, axis=1).astype(BF)
    hot = pair_hot(pair, width)
    return jnp.concatenate([top, jnp.where(hot, g2, 0.0).astype(BF)], axis=0)


def pair_hot(pair, width):
    x, y = pair_place(pair, width - 2)
    first = (x + 1) * width + y + 1
    lane = iota((L, 2 * L), 1)
    return iota((L, 2 * L), 0) == first + jnp.where(lane >= L, 1, 0)


def pair_rows(pair, width, ref):
    x, y = pair_place(pair, width - 2)
    first = (x + 1) * width + y + 1
    return ref[pl.ds(first, 1), :], ref[pl.ds(first + 1, 1), :]


def edges_forward(width, lhs_ref, weight_t_ref, far_ref, near_ref, shifts, g2, mid2_ref, bias2, sums_ref, wsum_ref):
    pairs = sums_ref.shape[0] // (2 * CAP)
    col = iota((CAP, EDGES), 1)
    start = iota((CAP, EDGES), 0) * NEAR
    own = mask((col >= start) & (col < start + NEAR))

    def body(pair, carry):
        rhs = pair_rhs(pair, width, far_ref, near_ref, shifts, g2)
        pre_one = dot(lhs_ref[...], rhs)
        hidden = (pre_one + pre_one * jnp.tanh(pre_one)).astype(BF)
        pre_two = dot(hidden, mid2_ref[...]) + bias2
        act = (pre_two + pre_two * jnp.tanh(pre_two)).astype(BF)
        row_a, row_b = pair_rows(pair, width, weight_t_ref)
        spread = jnp.concatenate([own * row_a, own * row_b], axis=0)
        sums = dot(spread.astype(BF), act)
        at = pl.ds(pl.multiple_of(pair * 2 * CAP, 2 * CAP), 2 * CAP)
        sums_ref[at, :] = jnp.concatenate([sums[:CAP, :L], sums[CAP:, L:]], axis=0)
        wsum_ref[at, :] = jnp.broadcast_to(jnp.sum(spread, axis=1, keepdims=True), (2 * CAP, L))
        return carry

    lax.fori_loop(0, pairs, body, 0)


def edges_backward(
    width, lhs_ref, weight_ref, radius_t_ref, hot_t_ref, far_ref, near_ref, shifts, g2, mid2_ref, mid2_t_ref, bias2,
    d_sums_ref, d_own_ref, d_far_ref, mid_ref, rows_ref, bias_ref,
):
    pairs = d_own_ref.shape[0] // (2 * CAP)
    d_far_ref[...] = jnp.zeros_like(d_far_ref)
    mid_ref[...] = jnp.zeros_like(mid_ref)
    rows_ref[...] = jnp.zeros_like(rows_ref)
    bias_ref[...] = jnp.zeros_like(bias_ref)

    def body(pair, carry):
        x, y = pair_place(pair, width - 2)
        rhs = pair_rhs(pair, width, far_ref, near_ref, shifts, g2)
        pre_one = dot(lhs_ref[...], rhs)
        tanh_one = jnp.tanh(pre_one)
        hidden = (pre_one + pre_one * tanh_one).astype(BF)
        pre_two = dot(hidden, mid2_ref[...]) + bias2
        pick = mask(pair_hot(pair, width)).astype(BF)
        weight = dot(weight_ref[...], pick)
        base = pl.multiple_of(pair * 2 * CAP, 2 * CAP)
        d_sums = d_sums_ref[pl.ds(base, 2 * CAP), :]
        d_sums = jnp.concatenate([d_sums[:CAP], d_sums[CAP:]], axis=1)
        d_sums = jnp.broadcast_to(d_sums[:, None, :], (CAP, NEAR, 2 * L)).reshape(EDGES, 2 * L)
        d_two = weight * d_sums * slope_of(pre_two, jnp.tanh(pre_two))
        bias_ref[...] += jnp.sum(d_two.reshape(EDGES // 8, 8, 2 * L), axis=0)
        d_two = d_two.astype(BF)
        mid_ref[...] += dot_tn(hidden, d_two)
        d_one = (dot(d_two, mid2_t_ref[...]) * slope_of(pre_one, tanh_one)).astype(BF)
        rad_a, rad_b = pair_rows(pair, width, radius_t_ref)
        tail = jnp.concatenate([rad_a, rad_b, jnp.zeros((14, EDGES), F32)], axis=0).astype(BF)
        back = dot(jnp.concatenate([hot_t_ref[...], tail], axis=0), d_one)
        rows_ref[...] += back
        own_rows = back[NEAR : NEAR + CAP]
        d_own_ref[pl.ds(base, 2 * CAP), :] = jnp.concatenate([own_rows[:, :L], own_rows[:, L:]], axis=0)
        for a in range(3):
            piece = back[3 * CAP * a : 3 * CAP * (a + 1)]
            zero = jnp.zeros((CAP, L), F32)
            both = jnp.concatenate([piece[:, :L], zero], axis=0) + jnp.concatenate([zero, piece[:, L:]], axis=0)
            at = pl.ds(pl.multiple_of(((x + a) * width + y) * CAP, CAP), 4 * CAP)
            d_far_ref[at, :] += both
        return carry

    lax.fori_loop(0, pairs, body, 0)


def geo_grads(rows, d_far, geo_halo, d_own, geo_own):
    def total(value):
        return jnp.sum(value, axis=0, keepdims=True)

    rows = jnp.concatenate([rows[: NEAR, :L] + rows[: NEAR, L:], rows[80:82, :L], rows[80:82, L:]], axis=0)
    block = [total(rows[CAP * k : CAP * (k + 1)]) for k in range(9)]
    grad_x = sum(float(k // 3 - 1) * block[k] for k in range(9) if k // 3 != 1)
    grad_y = sum(float(k % 3 - 1) * block[k] for k in range(9) if k % 3 != 1)
    grad_x = grad_x + total(column(geo_halo, 0) * d_far) - total(column(geo_own, 0) * d_own)
    grad_y = grad_y + total(column(geo_halo, 1) * d_far) - total(column(geo_own, 1) * d_own)
    grad_r = rows[NEAR : NEAR + 1] + rows[NEAR + 3 : NEAR + 4]
    return grad_x, grad_y, grad_r


def node_forward(latent, occ, sums, wsum, w_out, w_first, w_second, biases, gain):
    bias = biases.astype(F32)
    sums_low = sums.astype(BF)
    message_low = (dot(sums_low, w_out) + wsum * bias[1:2]).astype(BF)
    first_pre = dot(latent, w_first[:L]) + dot(message_low, w_first[L:]) + bias[2:3]
    half = 0.5 * first_pre
    first_low = (half + half * jnp.tanh(half)).astype(BF)
    second = dot(first_low, w_second) + bias[3:4]
    centred = second - jnp.mean(second, axis=1, keepdims=True)
    inv_root = lax.rsqrt(jnp.mean(centred * centred, axis=1, keepdims=True) + LN_EPS)
    normed = centred * inv_root
    update = normed * gain.astype(F32) + bias[4:5]
    new = (latent.astype(F32) + occ * update).astype(BF)
    return new, (sums_low, message_low, half, first_low, normed, inv_root)


def node_backward(d_new, latent, occ, wsum, saved, w_out, w_first, w_second, gain):
    sums_low, message_low, half, first_low, normed, inv_root = saved

    def total(value):
        return jnp.sum(value, axis=0, keepdims=True)

    d_update = occ * d_new
    grad_gain = total(d_update * normed)
    grad_shift = total(d_update)
    d_normed = d_update * gain.astype(F32)
    d_second = inv_root * (
        d_normed
        - jnp.mean(d_normed, axis=1, keepdims=True)
        - normed * jnp.mean(d_normed * normed, axis=1, keepdims=True)
    )
    d_second_low = d_second.astype(BF)
    grad_second = dot_tn(first_low, d_second_low)
    d_first = dot_nt(d_second_low, w_second) * slope_of(half, jnp.tanh(half))
    d_first_low = d_first.astype(BF)
    grad_first = [dot_tn(latent, d_first_low), dot_tn(message_low, d_first_low)]
    d_latent = dot_nt(d_first_low, w_first[:L])
    d_message = dot_nt(d_first_low, w_first[L:])
    d_message_low = d_message.astype(BF)
    grad_out = dot_tn(sums_low, d_message_low)
    d_sums = dot_nt(d_message_low, w_out)
    small = [total(wsum * d_message), total(d_first), total(d_second), grad_shift, grad_gain]
    return d_sums, d_latent, grad_out, grad_first, grad_second, small


def store_node_grads(grads_ref, small_ref, grad_out, grad_first, grad_second, small):
    base = L
    for block in (grad_out, grad_first[0], grad_first[1], grad_second):
        grads_ref[base : base + L, :] = block
        base += L
    small_ref[...] = jnp.concatenate(small + [jnp.zeros((3, L), F32)], axis=0)


def store_edge_grads(grads_ref, small_ref, mid, bias, geo):
    grads_ref[:L, :] = mid[:L, :L] + mid[L:, L:]
    bias = jnp.sum(bias, axis=0, keepdims=True)
    rows = [bias[:, :L] + bias[:, L:], small_ref[:5, :]] + list(geo)
    grads_ref[5 * L :, :] = jnp.concatenate(rows + [jnp.zeros((L - 9, L), F32)], axis=0)


def edge_constants(edge_geo_ref, mid_ref, biases_ref, mid2_ref, mid2_t_ref=None):
    edge_geo = edge_geo_ref[...]
    mid = mid_ref[...].astype(F32)
    mid2 = block_diag(0.5 * mid).astype(BF)
    bias2 = twice(0.5 * biases_ref[0:1, :].astype(F32))
    g2 = twice(0.5 * edge_geo[2:3].astype(F32))
    mid2_ref[...] = mid2
    if mid2_t_ref is not None:
        mid2_t_ref[...] = block_diag(mid.T).astype(BF)
    return shift_rows(edge_geo), g2, bias2


def first_kernel(
    width, halo_ref, pay_ref, own_ref, latent_ref, edge_geo_ref, mid_w_ref, out_w_ref, first_w_ref, second_w_ref,
    biases_ref, gain_ref, next_in_ref,
    lhs_ref, weight_ref, weight_t_ref, radius_t_ref, hot_t_ref, new_ref, next_own_ref, next_far_ref,
    wsum_ref, sums_low_ref, message_ref, half_ref, first_low_ref, normed_ref, inv_ref,
    far_ref, near_ref, sums_ref, mid2_ref,
):
    fill_geometry(halo_ref[:, L:], width, lhs_ref, weight_ref, weight_t_ref, radius_t_ref, hot_t_ref)
    fill_pre(halo_ref[:, :L], halo_ref[:, L:], own_ref[...], pay_ref[:, L:], edge_geo_ref[...], far_ref, near_ref)
    shifts, g2, bias2 = edge_constants(edge_geo_ref, mid_w_ref, biases_ref, mid2_ref)
    edges_forward(width, lhs_ref, weight_t_ref, far_ref, near_ref, shifts, g2, mid2_ref, bias2, sums_ref, wsum_ref)
    occ = column(pay_ref[:, L:], 2)
    new, saved = node_forward(
        latent_ref[...], occ, sums_ref[...], wsum_ref[...], out_w_ref[...], first_w_ref[...], second_w_ref[...],
        biases_ref[...], gain_ref[...],
    )
    for ref, value in zip((sums_low_ref, message_ref, half_ref, first_low_ref, normed_ref), saved):
        ref[...] = value
    inv_ref[...] = jnp.broadcast_to(saved[5], inv_ref.shape)
    new_ref[...] = new
    both = dot(new, next_in_ref[...])
    next_own_ref[...] = both[:, :L]
    next_far_ref[...] = both[:, L:].astype(BF)


def middle_kernel(
    width, far_in_ref, halo_ref, pay_ref, own_ref, latent_ref, cot_ref, lhs_ref, weight_ref, weight_t_ref,
    radius_t_ref, hot_t_ref, edge_geo_ref, mid_w_ref, out_w_ref, first_w_ref, second_w_ref, biases_ref, gain_ref,
    new_ref, d_own_ref, d_far_ref, grad_ref, grads_ref,
    far_ref, near_ref, sums_ref, wsum_ref, mid_ref, rows_ref, bias_ref, mid2_ref, mid2_t_ref, small_ref,
):
    fill_pre(far_in_ref[...], halo_ref[:, L:], own_ref[...], pay_ref[:, L:], edge_geo_ref[...], far_ref, near_ref)
    shifts, g2, bias2 = edge_constants(edge_geo_ref, mid_w_ref, biases_ref, mid2_ref, mid2_t_ref)
    edges_forward(width, lhs_ref, weight_t_ref, far_ref, near_ref, shifts, g2, mid2_ref, bias2, sums_ref, wsum_ref)
    occ = column(pay_ref[:, L:], 2)
    new, saved = node_forward(
        latent_ref[...], occ, sums_ref[...], wsum_ref[...], out_w_ref[...], first_w_ref[...], second_w_ref[...],
        biases_ref[...], gain_ref[...],
    )
    new_ref[...] = new
    d_new = cot_ref[...].astype(F32)
    d_sums, d_latent, grad_out, grad_first, grad_second, small = node_backward(
        d_new, latent_ref[...], occ, wsum_ref[...], saved, out_w_ref[...], first_w_ref[...], second_w_ref[...],
        gain_ref[...],
    )
    sums_ref[...] = d_sums
    grad_ref[...] = d_new + d_latent
    store_node_grads(grads_ref, small_ref, grad_out, grad_first, grad_second, small)
    edges_backward(
        width, lhs_ref, weight_ref, radius_t_ref, hot_t_ref, far_ref, near_ref, shifts, g2, mid2_ref, mid2_t_ref, bias2,
        sums_ref, d_own_ref, d_far_ref, mid_ref, rows_ref, bias_ref,
    )
    geo = geo_grads(rows_ref[...], d_far_ref[...], halo_ref[:, L:], d_own_ref[...], pay_ref[:, L:])
    store_edge_grads(grads_ref, small_ref, mid_ref[...], bias_ref[...], geo)


def back_kernel(
    width, next_d_own_ref, next_d_far_ref, next_grad_ref, next_latent_ref, next_in_ref, halo_ref, pay_ref, own_ref,
    latent_ref, lhs_ref, weight_ref, radius_t_ref, hot_t_ref, wsum_ref, sums_low_ref, message_ref, half_ref,
    first_low_ref, normed_ref, inv_ref,
    edge_geo_ref, mid_w_ref, out_w_ref, first_w_ref, second_w_ref, biases_ref, gain_ref,
    d_own_ref, d_far_ref, grad_ref, grads_ref, grad_in_ref,
    far_ref, near_ref, sums_ref, mid_ref, rows_ref, bias_ref, mid2_ref, mid2_t_ref, small_ref,
):
    d_both = jnp.concatenate([next_d_own_ref[...], next_d_far_ref[...]], axis=1).astype(BF)
    grad_in_ref[...] = dot_tn(next_latent_ref[...], d_both)
    d_new = next_grad_ref[...] + dot_nt(d_both, next_in_ref[...])
    fill_pre(halo_ref[:, :L], halo_ref[:, L:], own_ref[...], pay_ref[:, L:], edge_geo_ref[...], far_ref, near_ref)
    shifts, g2, bias2 = edge_constants(edge_geo_ref, mid_w_ref, biases_ref, mid2_ref, mid2_t_ref)
    occ = column(pay_ref[:, L:], 2)
    saved = (
        sums_low_ref[...], message_ref[...], half_ref[...], first_low_ref[...], normed_ref[...], inv_ref[...],
    )
    d_sums, d_latent, grad_out, grad_first, grad_second, small = node_backward(
        d_new, latent_ref[...], occ, wsum_ref[...], saved, out_w_ref[...], first_w_ref[...], second_w_ref[...],
        gain_ref[...],
    )
    sums_ref[...] = d_sums
    grad_ref[...] = d_new + d_latent
    store_node_grads(grads_ref, small_ref, grad_out, grad_first, grad_second, small)
    edges_backward(
        width, lhs_ref, weight_ref, radius_t_ref, hot_t_ref, far_ref, near_ref, shifts, g2, mid2_ref, mid2_t_ref, bias2,
        sums_ref, d_own_ref, d_far_ref, mid_ref, rows_ref, bias_ref,
    )
    geo = geo_grads(rows_ref[...], d_far_ref[...], halo_ref[:, L:], d_own_ref[...], pay_ref[:, L:])
    store_edge_grads(grads_ref, small_ref, mid_ref[...], bias_ref[...], geo)


def last_kernel(d_own_ref, d_far_ref, grad_ref, latent_ref, edge_in_ref, pay_ref, out_ref, grad_in_ref):
    d_both = jnp.concatenate([d_own_ref[...], d_far_ref[...]], axis=1).astype(BF)
    grad_in_ref[...] = dot_tn(latent_ref[...], d_both)
    occ = column(pay_ref[:, L:], 2)
    out_ref[...] = occ * (grad_ref[...] + dot_nt(d_both, edge_in_ref[...]))


def call(kernel, outs, scratch, *args):
    return pl.pallas_call(
        kernel,
        out_shape=[jax.ShapeDtypeStruct(shape, dtype) for shape, dtype in outs],
        in_specs=[pl.BlockSpec(memory_space=pltpu.VMEM)] * len(args),
        out_specs=[pl.BlockSpec(memory_space=pltpu.VMEM)] * len(outs),
        scratch_shapes=[pltpu.VMEM(shape, dtype) for shape, dtype in scratch],
        compiler_params=pltpu.CompilerParams(vmem_limit_bytes=48 * 1024 * 1024),
    )(*args)


def from_behind(value, axis, steps):
    count = lax.axis_size(axis)
    return lax.ppermute(value, axis, [(source, (source + steps) % count) for source in range(count)])


def with_halo(block):
    for axis, dim in (("gx", 0), ("gy", 1)):
        size = block.shape[dim]
        low = from_behind(lax.slice_in_dim(block, size - 1, size, axis=dim), axis, 1)
        high = from_behind(lax.slice_in_dim(block, 0, 1, axis=dim), axis, -1)
        block = jnp.concatenate([low, block, high], axis=dim)
    return block


def fold_halo(block):
    for axis, dim in (("gx", 0), ("gy", 1)):
        size = block.shape[dim]
        high = from_behind(lax.slice_in_dim(block, 0, 1, axis=dim).astype(BF), axis, -1).astype(F32)
        low = from_behind(lax.slice_in_dim(block, size - 1, size, axis=dim).astype(BF), axis, 1).astype(F32)
        inner = lax.slice_in_dim(block, 1, size - 1, axis=dim)
        first = lax.slice_in_dim(inner, 0, 1, axis=dim) + low
        last = lax.slice_in_dim(inner, size - 3, size - 2, axis=dim) + high
        block = jnp.concatenate([first, lax.slice_in_dim(inner, 1, size - 3, axis=dim), last], axis=dim)
    return block


def total_over_devices(rows):
    axes = ("gx", "gy")
    count = lax.axis_size("gx") * lax.axis_size("gy")
    parts = lax.all_to_all(rows.astype(BF).reshape(count, -1, L), axes, 0, 0)
    mine = jnp.sum(parts.astype(F32), axis=0).astype(BF)
    spread = jnp.broadcast_to(mine[None], (count,) + mine.shape)
    return lax.all_to_all(spread, axes, 0, 0).reshape(-1, L).astype(F32)


def on_device(
    latent, offset, owner, slot, cotangent, edge_in, edge_geo, edge_mid, edge_out, node_in, node_out, biases, ln_gain
):
    cells_x, cells_y, cap_size, width_l = cotangent.shape
    slots = cells_x * cells_y * cap_size
    width = cells_y + 2
    halo_rows = (cells_x + 2) * width * cap_size
    count_x = lax.axis_size("gx")
    count_y = lax.axis_size("gy")
    my_x = lax.axis_index("gx")
    my_y = lax.axis_index("gy")
    rows = latent.shape[0]
    send = rows // 9
    step_x = (owner // count_y - my_x + 1) % count_x
    step_y = (owner % count_y - my_y + 1) % count_y
    bucket = (step_x * 3 + step_y)[None, :]
    mark = slot + 1
    ones = jnp.ones((rows,), F32)
    zeros = jnp.zeros((rows,), F32)
    meta = jnp.stack(
        [
            offset[0].astype(F32), offset[1].astype(F32), ones, (mark // 16).astype(F32), (mark % 16).astype(F32),
            zeros, zeros, zeros,
        ]
    )
    (sent,) = call(sort_kernel, [((rows, 2 * L), BF)], [], latent, bucket, meta)
    sent = sent.reshape(3, 3, send, 2 * L)
    sections = [sent[:, 1], from_behind(sent[:, 2], "gy", 1), from_behind(sent[:, 0], "gy", -1)]
    section = jnp.stack(sections)
    final = [section[:, 1], from_behind(section[:, 2], "gx", 1), from_behind(section[:, 0], "gx", -1)]
    arrived = jnp.concatenate([piece.reshape(-1, 2 * L) for piece in final], axis=0)
    v0, own0, pay = call(
        place_kernel, [((slots, L), BF), ((slots, L), F32), ((slots, 2 * L), BF)], [], arrived, edge_in[0]
    )
    halo = with_halo(pay.reshape(cells_x, cells_y, cap_size, 2 * L)).reshape(halo_rows, 2 * L)

    def weights(t):
        return (edge_geo[t], edge_mid[t], edge_out[t], node_in[t], node_out[t], biases[t], ln_gain[t][None, :])

    node = ((slots, L), F32)
    node_low = ((slots, L), BF)
    geometry = [((EDGES, 2 * L), BF), ((EDGES, L), BF), ((L, EDGES), F32), ((L, EDGES), F32), ((80, EDGES), BF)]
    edge_scratch = [((halo_rows, L), F32), node, node]
    sums_scratch = [((2 * L, 2 * L), F32), ((96, 2 * L), F32), ((8, 2 * L), F32)]
    sums_scratch += [((2 * L, 2 * L), BF)] * 2 + [((8, L), F32)]
    firsts = call(
        functools.partial(first_kernel, width),
        geometry + [node_low, node, node_low, node, node_low, node_low, node, node_low, node, node],
        edge_scratch + [((2 * L, 2 * L), BF)],
        halo, pay, own0, v0, *weights(0), edge_in[1],
    )
    lhs, weight, weight_t, radius_t, hot_t = firsts[:5]
    v1, own1, far1 = firsts[5:8]
    saved0 = firsts[8:]
    far1_halo = with_halo(far1.reshape(cells_x, cells_y, cap_size, L)).reshape(halo_rows, L)
    edge_outs = [node, ((halo_rows, L), F32), node, ((768, L), F32)]
    v2, d_own1, d_far1, grad1, grads1 = call(
        functools.partial(middle_kernel, width),
        [node_low] + edge_outs,
        edge_scratch + [node] + sums_scratch,
        far1_halo, halo, pay, own1, v1, cotangent.reshape(slots, L), lhs, weight, weight_t, radius_t, hot_t, *weights(1),
    )
    d_far1 = fold_halo(d_far1.reshape(cells_x + 2, width, cap_size, L)).reshape(slots, L)
    d_own0, d_far0, grad0, grads0, grad_in1 = call(
        functools.partial(back_kernel, width),
        edge_outs + [((L, 2 * L), F32)],
        edge_scratch + sums_scratch,
        d_own1, d_far1, grad1, v1, edge_in[1], halo, pay, own0, v0, lhs, weight, radius_t, hot_t, *saved0, *weights(0),
    )
    d_far0 = fold_halo(d_far0.reshape(cells_x + 2, width, cap_size, L)).reshape(slots, L)
    latent_grad, grad_in0 = call(
        last_kernel, [node, ((L, 2 * L), F32)], [], d_own0, d_far0, grad0, v0, edge_in[0], pay
    )
    packed = jnp.concatenate(
        [
            grad_in0[:, :L], grad_in0[:, L:], grads0, grad_in1[:, :L], grad_in1[:, L:], grads1,
        ],
        axis=0,
    )
    total = total_over_devices(packed) * (float(slots * count_x * count_y) ** -0.5)
    total = total.reshape(STEPS, GROWS, L)
    cells = (cells_x, cells_y, cap_size, width_l)
    return (
        v2.reshape(cells),
        latent_grad.reshape(cells),
        jnp.concatenate([total[:, :L], total[:, L : 2 * L]], axis=2),
        total[:, 902:905],
        total[:, 2 * L : 3 * L],
        total[:, 3 * L : 4 * L],
        total[:, 4 * L : 6 * L],
        total[:, 6 * L : 7 * L],
        total[:, 896:901],
        total[:, 901],
    )


def solution(mesh):
    rows = P(("gx", "gy"))
    grid = P("gx", "gy", None, None)
    in_specs = (P(("gx", "gy"), None), P(None, ("gx", "gy")), rows, rows, grid) + (P(),) * 8
    out_specs = (grid, grid) + (P(),) * 8
    return jax.shard_map(on_device, mesh=mesh, in_specs=in_specs, out_specs=out_specs, check_vma=False)
```

```python
import functools

import jax
import jax.numpy as jnp
from jax import lax
from jax.experimental import pallas as pl
from jax.experimental.pallas import tpu as pltpu
from jax.sharding import PartitionSpec as P

STEPS = 2
LN_EPS = 1e-05
F32 = jnp.float32
BF = jnp.bfloat16
L = 128
CAP = 8
NEAR = 9 * CAP
EDGES = CAP * NEAR
GROWS = 1024


def dot(a, b):
    return jnp.dot(a, b, preferred_element_type=F32)


def dot_tn(a, b):
    return lax.dot_general(a, b, (((0,), (0,)), ((), ())), preferred_element_type=F32)


def dot_nt(a, b):
    return lax.dot_general(a, b, (((1,), (1,)), ((), ())), preferred_element_type=F32)


def iota(shape, dim):
    return lax.broadcasted_iota(jnp.int32, shape, dim)


def mask(cond):
    return jnp.where(cond, 1.0, 0.0).astype(F32)


def slope_of(half, tanh_half):
    sig = 0.5 + 0.5 * tanh_half
    act = half + half * tanh_half
    return sig + act * (1.0 - sig)


def sort_kernel(latent_ref, bucket_ref, meta_ref, out_ref):
    rows = latent_ref.shape[0]
    send = rows // 9
    bucket = bucket_ref[...]
    hot = mask(iota((16, rows), 0) == bucket)
    upper = mask(iota((rows, rows), 0) <= iota((rows, rows), 1)).astype(BF)
    count = dot(hot.astype(BF), upper)
    rank = jnp.sum(hot * (count - 1.0), axis=0, keepdims=True)
    target = bucket.astype(F32) * float(send) + rank
    perm = mask(iota((rows, rows), 0).astype(F32) == target).astype(BF)
    out_ref[:, :L] = dot(perm, latent_ref[...]).astype(BF)
    meta = jnp.concatenate([meta_ref[...], jnp.zeros((L - 8, rows), F32)], axis=0).astype(BF)
    out_ref[:, L:] = dot_nt(perm, meta).astype(BF)


def place_kernel(rows_ref, pay_ref):
    rows = rows_ref.shape[0]
    slots = pay_ref.shape[0]
    pick_lane = iota((8, L), 1)
    pick = jnp.where(pick_lane == 3, 16.0, jnp.where(pick_lane == 4, 1.0, 0.0)).astype(BF)
    mark = dot_nt(pick, rows_ref[:, L:])[0:1]
    hot = mask((iota((slots, rows), 0) + 1).astype(F32) == mark).astype(BF)
    pay_ref[...] = dot(hot, rows_ref[...]).astype(BF)


def fill_geometry(geo, width, lhs_ref, weight_ref, weight_t_ref, radius_t_ref, hot_t_ref):
    halo_rows = geo.shape[0]
    rows = dot_nt(mask(iota((8, L), 0) == iota((8, L), 1)).astype(BF), geo)
    cell = iota((halo_rows, L), 1) * CAP
    row = iota((halo_rows, L), 0)
    cell_hot = mask((row >= cell) & (row < cell + CAP)).astype(BF)
    slot_hot = mask((iota((8, halo_rows), 1) & (CAP - 1)) == iota((8, halo_rows), 0))
    px, py, occ = (dot((slot_hot * rows[k : k + 1]).astype(BF), cell_hot) for k in range(3))
    near = ([], [], [])
    for a in (-1, 0, 1):
        for b in (-1, 0, 1):
            shift = (-(width * a + b)) % L
            for piece, value, base in zip(near, (px, py, occ), (a, b, 0)):
                moved = value if shift == 0 else pltpu.roll(value, shift, 1)
                piece.append(moved + float(base))
    near_x, near_y, near_occ = (jnp.concatenate(piece, axis=0) for piece in near)
    radius, weight, hots = [], [], []
    lane = iota((NEAR, L), 1)
    sub = iota((NEAR, L), 0)
    for i in range(CAP):
        dx = near_x - px[i : i + 1]
        dy = near_y - py[i : i + 1]
        r2 = dx * dx + dy * dy
        reach = jnp.maximum(1.0 - r2, 0.0)
        w = occ[i : i + 1] * near_occ * reach * reach
        radius.append(r2)
        weight.append(jnp.where(sub == 4 * CAP + i, 0.0, w))
        hots.append(mask((sub == lane) | (lane == NEAR + i) | (lane == NEAR + CAP + i)))
    radius = jnp.concatenate(radius, axis=0)
    weight = jnp.concatenate(weight, axis=0)
    hots = jnp.concatenate(hots, axis=0)
    lhs_ref[:, :L] = hots.astype(BF)
    lhs_ref[:, L:] = radius.astype(BF)
    weight_ref[...] = weight.astype(BF)
    weight_t_ref[...] = weight.T
    radius_t_ref[...] = radius.T
    hot_t_ref[...] = hots.T[:80].astype(BF)


def column(value, k):
    return value[:, k : k + 1].astype(F32)


def fill_pre(far, geo_halo, own, geo_own, edge_geo, far_ref, near_ref):
    g0 = 0.5 * edge_geo[0:1].astype(F32)
    g1 = 0.5 * edge_geo[1:2].astype(F32)
    far_ref[...] = 0.5 * far.astype(F32) + column(geo_halo, 0) * g0 + column(geo_halo, 1) * g1
    near_ref[...] = 0.5 * own - column(geo_own, 0) * g0 - column(geo_own, 1) * g1


def shift_rows(edge_geo):
    g0 = 0.5 * edge_geo[0:1].astype(F32)
    g1 = 0.5 * edge_geo[1:2].astype(F32)
    side = iota((3 * CAP, L), 0) // CAP - 1
    return [float(a) * g0 + side.astype(F32) * g1 for a in (-1, 0, 1)]


def twice(row):
    return jnp.concatenate([row, row], axis=1)


def block_diag(w):
    zero = jnp.zeros_like(w)
    return jnp.concatenate(
        [jnp.concatenate([w, zero], axis=1), jnp.concatenate([zero, w], axis=1)], axis=0
    )


def pair_place(pair, cells_y):
    half = cells_y // 2
    x = pair // half
    y = (pair - x * half) * 2
    return x, y


def pair_rhs(pair, width, far_ref, near_ref, shifts, g2):
    x, y = pair_place(pair, width - 2)
    tops = []
    for k in range(2):
        pieces = []
        for a in range(3):
            start = pl.multiple_of(((x + a) * width + y + k) * CAP, CAP)
            pieces.append(far_ref[pl.ds(start, 3 * CAP), :] + shifts[a])
        mine = near_ref[pl.ds(pl.multiple_of((pair * 2 + k) * CAP, CAP), CAP), :]
        pieces.append(mine)
        pieces.append(mine - mine.astype(BF).astype(F32))
        pieces.append(jnp.zeros((L - NEAR - 2 * CAP, L), F32))
        tops.append(jnp.concatenate(pieces, axis=0))
    top = jnp.concatenate(tops, axis=1).astype(BF)
    hot = pair_hot(pair, width)
    return jnp.concatenate([top, jnp.where(hot, g2, 0.0).astype(BF)], axis=0)


def pair_hot(pair, width):
    x, y = pair_place(pair, width - 2)
    first = (x + 1) * width + y + 1
    lane = iota((L, 2 * L), 1)
    return iota((L, 2 * L), 0) == first + jnp.where(lane >= L, 1, 0)


def pair_rows(pair, width, ref):
    x, y = pair_place(pair, width - 2)
    first = (x + 1) * width + y + 1
    return ref[pl.ds(first, 1), :], ref[pl.ds(first + 1, 1), :]


def edges_forward(
    width, lhs_ref, weight_t_ref, far_ref, near_ref, shifts, g2, mid2_ref, bias2, sums_ref, wsum_ref, keep=None
):
    pairs = sums_ref.shape[0] // (2 * CAP)
    col = iota((CAP, EDGES), 1)
    start = iota((CAP, EDGES), 0) * NEAR
    own = mask((col >= start) & (col < start + NEAR))

    def body(pair, carry):
        rhs = pair_rhs(pair, width, far_ref, near_ref, shifts, g2)
        pre_one = dot(lhs_ref[...], rhs).astype(BF)
        tanh_one = jnp.tanh(pre_one)
        hidden = pre_one + pre_one * tanh_one
        pre_two = (dot(hidden, mid2_ref[...]) + bias2).astype(BF)
        tanh_two = jnp.tanh(pre_two)
        act = pre_two + pre_two * tanh_two
        if keep is not None:
            at = pl.ds(pl.multiple_of(pair * EDGES, EDGES), EDGES)
            keep[0][at, :] = hidden
            keep[1][at, :] = slope_of(pre_one, tanh_one)
            keep[2][at, :] = slope_of(pre_two, tanh_two)
        row_a, row_b = pair_rows(pair, width, weight_t_ref)
        spread = jnp.concatenate([own * row_a, own * row_b], axis=0)
        sums = dot(spread.astype(BF), act)
        at = pl.ds(pl.multiple_of(pair * 2 * CAP, 2 * CAP), 2 * CAP)
        sums_ref[at, :] = jnp.concatenate([sums[:CAP, :L], sums[CAP:, L:]], axis=0)
        wsum_ref[at, :] = jnp.broadcast_to(jnp.sum(spread, axis=1, keepdims=True), (2 * CAP, L))
        return carry

    lax.fori_loop(0, pairs, body, 0, unroll=4)


def edges_backward(
    width, lhs_ref, weight_ref, radius_t_ref, hot_t_ref, far_ref, near_ref, shifts, g2, mid2_ref, mid2_t_ref, bias2,
    d_sums_ref, d_own_ref, d_far_ref, mid_ref, rows_ref, bias_ref, keep=None,
):
    pairs = d_own_ref.shape[0] // (2 * CAP)
    for ref in (d_far_ref, mid_ref, rows_ref, bias_ref):
        ref[...] = jnp.zeros_like(ref)

    def body(pair, carry):
        x, y = pair_place(pair, width - 2)
        if keep is None:
            rhs = pair_rhs(pair, width, far_ref, near_ref, shifts, g2)
            pre_one = dot(lhs_ref[...], rhs).astype(BF)
            tanh_one = jnp.tanh(pre_one)
            hidden = pre_one + pre_one * tanh_one
            pre_two = (dot(hidden, mid2_ref[...]) + bias2).astype(BF)
            slope_one = slope_of(pre_one, tanh_one)
            slope_two = slope_of(pre_two, jnp.tanh(pre_two))
        else:
            at = pl.ds(pl.multiple_of(pair * EDGES, EDGES), EDGES)
            hidden, slope_one, slope_two = (ref[at, :] for ref in keep)
        pick = mask(pair_hot(pair, width)).astype(BF)
        weight = dot(weight_ref[...], pick)
        base = pl.multiple_of(pair * 2 * CAP, 2 * CAP)
        d_sums = d_sums_ref[pl.ds(base, 2 * CAP), :]
        d_sums = jnp.concatenate([d_sums[:CAP], d_sums[CAP:]], axis=1)
        d_sums = jnp.broadcast_to(d_sums[:, None, :], (CAP, NEAR, 2 * L)).reshape(EDGES, 2 * L)
        d_two = weight * d_sums * slope_two
        bias_ref[...] += jnp.sum(d_two.reshape(EDGES // 8, 8, 2 * L), axis=0)
        d_two = d_two.astype(BF)
        mid_ref[...] += dot_tn(hidden, d_two)
        d_one = (dot(d_two, mid2_t_ref[...]) * slope_one).astype(BF)
        rad_a, rad_b = pair_rows(pair, width, radius_t_ref)
        tail = jnp.concatenate([rad_a, rad_b, jnp.zeros((14, EDGES), F32)], axis=0).astype(BF)
        back = dot(jnp.concatenate([hot_t_ref[...], tail], axis=0), d_one)
        rows_ref[...] += back
        own_rows = back[NEAR : NEAR + CAP]
        d_own_ref[pl.ds(base, 2 * CAP), :] = jnp.concatenate([own_rows[:, :L], own_rows[:, L:]], axis=0)
        for a in range(3):
            piece = back[3 * CAP * a : 3 * CAP * (a + 1)]
            zero = jnp.zeros((CAP, L), F32)
            both = jnp.concatenate([piece[:, :L], zero], axis=0) + jnp.concatenate([zero, piece[:, L:]], axis=0)
            at = pl.ds(pl.multiple_of(((x + a) * width + y) * CAP, CAP), 4 * CAP)
            d_far_ref[at, :] += both
        return carry

    lax.fori_loop(0, pairs, body, 0, unroll=4)


def geo_grads(rows, d_far, geo_halo, d_own, geo_own):
    def total(value):
        return jnp.sum(value, axis=0, keepdims=True)

    rows = jnp.concatenate([rows[: NEAR, :L] + rows[: NEAR, L:], rows[80:82, :L], rows[80:82, L:]], axis=0)
    block = [total(rows[CAP * k : CAP * (k + 1)]) for k in range(9)]
    grad_x = sum(float(k // 3 - 1) * block[k] for k in range(9) if k // 3 != 1)
    grad_y = sum(float(k % 3 - 1) * block[k] for k in range(9) if k % 3 != 1)
    grad_x = grad_x + total(column(geo_halo, 0) * d_far) - total(column(geo_own, 0) * d_own)
    grad_y = grad_y + total(column(geo_halo, 1) * d_far) - total(column(geo_own, 1) * d_own)
    grad_r = rows[NEAR : NEAR + 1] + rows[NEAR + 3 : NEAR + 4]
    return grad_x, grad_y, grad_r


def node_forward(latent, occ, sums, wsum, w_out, w_first, w_second, biases, gain):
    bias = biases.astype(F32)
    sums_low = sums.astype(BF)
    message_low = (dot(sums_low, w_out) + wsum * bias[1:2]).astype(BF)
    first_pre = dot(latent, w_first[:L]) + dot(message_low, w_first[L:]) + bias[2:3]
    half = 0.5 * first_pre
    first_low = (half + half * jnp.tanh(half)).astype(BF)
    second = dot(first_low, w_second) + bias[3:4]
    centred = second - jnp.mean(second, axis=1, keepdims=True)
    inv_root = lax.rsqrt(jnp.mean(centred * centred, axis=1, keepdims=True) + LN_EPS)
    normed = centred * inv_root
    update = normed * gain.astype(F32) + bias[4:5]
    new = (latent.astype(F32) + occ * update).astype(BF)
    return new, (sums_low, message_low, half, first_low, normed, inv_root)


def node_backward(d_new, latent, occ, wsum, saved, w_out, w_first, w_second, gain):
    sums_low, message_low, half, first_low, normed, inv_root = saved

    def total(value):
        return jnp.sum(value, axis=0, keepdims=True)

    d_update = occ * d_new
    grad_gain = total(d_update * normed)
    grad_shift = total(d_update)
    d_normed = d_update * gain.astype(F32)
    d_second = inv_root * (
        d_normed
        - jnp.mean(d_normed, axis=1, keepdims=True)
        - normed * jnp.mean(d_normed * normed, axis=1, keepdims=True)
    )
    d_second_low = d_second.astype(BF)
    grad_second = dot_tn(first_low, d_second_low)
    d_first = dot_nt(d_second_low, w_second) * slope_of(half, jnp.tanh(half))
    d_first_low = d_first.astype(BF)
    grad_first = [dot_tn(latent, d_first_low), dot_tn(message_low, d_first_low)]
    d_latent = dot_nt(d_first_low, w_first[:L])
    d_message = dot_nt(d_first_low, w_first[L:])
    d_message_low = d_message.astype(BF)
    grad_out = dot_tn(sums_low, d_message_low)
    d_sums = dot_nt(d_message_low, w_out)
    small = [total(wsum * d_message), total(d_first), total(d_second), grad_shift, grad_gain]
    return d_sums, d_latent, grad_out, grad_first, grad_second, small


def store_node_grads(grads_ref, small_ref, grad_out, grad_first, grad_second, small):
    base = 3 * L
    for block in (grad_out, grad_first[0], grad_first[1], grad_second):
        grads_ref[base : base + L, :] = block.astype(BF)
        base += L
    small_ref[...] = jnp.concatenate(small + [jnp.zeros((3, L), F32)], axis=0)


def store_edge_grads(grads_ref, small_ref, latent, latent_halo, d_own, d_far, mid, bias, geo):
    grads_ref[:L, :] = dot_tn(latent, d_own.astype(BF)).astype(BF)
    grads_ref[L : 2 * L, :] = dot_tn(latent_halo, d_far.astype(BF)).astype(BF)
    grads_ref[2 * L : 3 * L, :] = (mid[:L, :L] + mid[L:, L:]).astype(BF)
    bias = jnp.sum(bias, axis=0, keepdims=True)
    rows = [bias[:, :L] + bias[:, L:], small_ref[:5, :]] + list(geo)
    grads_ref[7 * L :, :] = jnp.concatenate(rows + [jnp.zeros((L - 9, L), F32)], axis=0).astype(BF)


class Step:
    def __init__(self, refs, t):
        names = ("edge_in", "edge_geo", "edge_mid", "edge_out", "node_in", "node_out", "biases")
        for name, ref in zip(names, refs):
            setattr(self, name, ref[t])
        self.gain = refs[7][t : t + 1, :]


def prepare(w, latent_halo, geo_halo, latent, geo_own, far_ref, near_ref, mid2_ref, mid2_t_ref=None):
    far = dot(latent_halo, w.edge_in[:, L:]).astype(BF)
    own = dot(latent, w.edge_in[:, :L])
    fill_pre(far, geo_halo, own, geo_own, w.edge_geo, far_ref, near_ref)
    mid = w.edge_mid.astype(F32)
    mid2_ref[...] = block_diag(0.5 * mid).astype(BF)
    if mid2_t_ref is not None:
        mid2_t_ref[...] = block_diag(mid.T).astype(BF)
    bias2 = twice(0.5 * w.biases[0:1].astype(F32))
    g2 = twice(0.5 * w.edge_geo[2:3].astype(F32))
    return shift_rows(w.edge_geo), g2, bias2


def first_kernel(width, halo_ref, pay_ref, *refs):
    w = Step(refs[:8], 0)
    lhs_ref, weight_ref, weight_t_ref, radius_t_ref, hot_t_ref, new_ref, wsum_ref = refs[8:15]
    saved_refs = refs[15:20]
    inv_ref, far_ref, near_ref, sums_ref, mid2_ref = refs[20:]
    fill_geometry(halo_ref[:, L:], width, lhs_ref, weight_ref, weight_t_ref, radius_t_ref, hot_t_ref)
    latent, geo_own = pay_ref[:, :L], pay_ref[:, L:]
    shifts, g2, bias2 = prepare(
        w, halo_ref[:, :L], halo_ref[:, L:], latent, geo_own, far_ref, near_ref, mid2_ref
    )
    edges_forward(width, lhs_ref, weight_t_ref, far_ref, near_ref, shifts, g2, mid2_ref, bias2, sums_ref, wsum_ref)
    new, saved = node_forward(
        pay_ref[:, :L], column(pay_ref[:, L:], 2), sums_ref[...], wsum_ref[...], w.edge_out, w.node_in, w.node_out,
        w.biases, w.gain,
    )
    for ref, value in zip(saved_refs, saved):
        ref[...] = value
    inv_ref[...] = jnp.broadcast_to(saved[5], inv_ref.shape)
    new_ref[...] = new


def backward(
    width, w, d_new, latent_halo_ref, latent_ref, halo_ref, pay_ref, saved, wsum_ref, geometry, consts, outs, scratch, keep
):
    lhs_ref, weight_ref, radius_t_ref, hot_t_ref = geometry
    d_own_ref, d_far_ref, grad_ref, grads_ref = outs
    far_ref, near_ref, sums_ref, mid_ref, rows_ref, bias_ref, mid2_ref, mid2_t_ref, small_ref = scratch
    shifts, g2, bias2 = consts
    d_sums, d_latent, grad_out, grad_first, grad_second, small = node_backward(
        d_new, latent_ref[:, :L], column(pay_ref[:, L:], 2), wsum_ref[...], saved, w.edge_out, w.node_in, w.node_out,
        w.gain,
    )
    sums_ref[...] = d_sums
    grad_ref[...] = d_new + d_latent
    store_node_grads(grads_ref, small_ref, grad_out, grad_first, grad_second, small)
    edges_backward(
        width, lhs_ref, weight_ref, radius_t_ref, hot_t_ref, far_ref, near_ref, shifts, g2, mid2_ref, mid2_t_ref, bias2,
        sums_ref, d_own_ref, d_far_ref, mid_ref, rows_ref, bias_ref, keep,
    )
    geo = geo_grads(rows_ref[...], d_far_ref[...], halo_ref[:, L:], d_own_ref[...], pay_ref[:, L:])
    store_edge_grads(
        grads_ref, small_ref, latent_ref[:, :L], latent_halo_ref[:, :L], d_own_ref[...], d_far_ref[...], mid_ref[...],
        bias_ref[...], geo,
    )


def middle_kernel(width, latent_halo_ref, halo_ref, pay_ref, latent_ref, cot_ref, *refs):
    lhs_ref, weight_ref, weight_t_ref, radius_t_ref, hot_t_ref = refs[:5]
    w = Step(refs[5:13], 1)
    new_ref = refs[13]
    outs = refs[14:18]
    scratch = refs[18:27]
    wsum_ref = refs[27]
    keep = refs[28:]
    far_ref, near_ref, sums_ref = scratch[:3]
    mid2_ref, mid2_t_ref = scratch[6:8]
    consts = prepare(
        w, latent_halo_ref[...], halo_ref[:, L:], latent_ref[...], pay_ref[:, L:], far_ref, near_ref, mid2_ref, mid2_t_ref
    )
    shifts, g2, bias2 = consts
    edges_forward(
        width, lhs_ref, weight_t_ref, far_ref, near_ref, shifts, g2, mid2_ref, bias2, sums_ref, wsum_ref, keep
    )
    new, saved = node_forward(
        latent_ref[...], column(pay_ref[:, L:], 2), sums_ref[...], wsum_ref[...], w.edge_out, w.node_in, w.node_out,
        w.biases, w.gain,
    )
    new_ref[...] = new
    backward(
        width, w, cot_ref[...].astype(F32), latent_halo_ref, latent_ref, halo_ref, pay_ref, saved, wsum_ref,
        (lhs_ref, weight_ref, radius_t_ref, hot_t_ref), consts, outs, scratch, keep,
    )


def back_kernel(width, next_d_own_ref, next_d_far_ref, next_grad_ref, halo_ref, pay_ref, *refs):
    lhs_ref, weight_ref, radius_t_ref, hot_t_ref, wsum_ref = refs[:5]
    saved = tuple(ref[...] for ref in refs[5:11])
    w = Step(refs[11:19], 0)
    outs = refs[19:23]
    scratch = refs[23:]
    d_both = jnp.concatenate([next_d_own_ref[...], next_d_far_ref[...]], axis=1).astype(BF)
    d_new = next_grad_ref[...] + dot_nt(d_both, refs[11][1])
    consts = prepare(
        w, halo_ref[:, :L], halo_ref[:, L:], pay_ref[:, :L], pay_ref[:, L:], *scratch[:2], *scratch[6:8]
    )
    backward(
        width, w, d_new, halo_ref, pay_ref, halo_ref, pay_ref, saved, wsum_ref,
        (lhs_ref, weight_ref, radius_t_ref, hot_t_ref), consts, outs, scratch, None,
    )


def last_kernel(d_own_ref, d_far_ref, grad_ref, edge_in_ref, pay_ref, out_ref):
    d_both = jnp.concatenate([d_own_ref[...], d_far_ref[...]], axis=1).astype(BF)
    out_ref[...] = column(pay_ref[:, L:], 2) * (grad_ref[...] + dot_nt(d_both, edge_in_ref[0]))


def unpack_kernel(scale, rows_ref, in_ref, geo_ref, mid_ref, out_ref, first_ref, second_ref, bias_ref, gain_ref):
    gains = []
    for t in range(STEPS):
        def take(start, size, base=t * GROWS):
            return rows_ref[base + start : base + start + size, :].astype(F32) * scale

        in_ref[t, :, :L] = take(0, L)
        in_ref[t, :, L:] = take(L, L)
        mid_ref[t] = take(2 * L, L)
        out_ref[t] = take(3 * L, L)
        first_ref[t] = take(4 * L, 2 * L)
        second_ref[t] = take(6 * L, L)
        small = take(7 * L, 16)
        bias_ref[t] = small[:5]
        geo_ref[t] = small[6:9]
        gains.append(small[5:6])
    gain_ref[...] = jnp.concatenate(gains, axis=0)


def call(kernel, outs, scratch, *args, mib=8):
    return pl.pallas_call(
        kernel,
        out_shape=[jax.ShapeDtypeStruct(shape, dtype) for shape, dtype in outs],
        in_specs=[pl.BlockSpec(memory_space=pltpu.VMEM)] * len(args),
        out_specs=[pl.BlockSpec(memory_space=pltpu.VMEM)] * len(outs),
        scratch_shapes=[pltpu.VMEM(shape, dtype) for shape, dtype in scratch],
        compiler_params=pltpu.CompilerParams(vmem_limit_bytes=mib * 1024 * 1024),
    )(*args)


def from_behind(value, axis, steps):
    count = lax.axis_size(axis)
    return lax.ppermute(value, axis, [(source, (source + steps) % count) for source in range(count)])


def with_halo(block):
    for axis, dim in (("gx", 0), ("gy", 1)):
        size = block.shape[dim]
        low = from_behind(lax.slice_in_dim(block, size - 1, size, axis=dim), axis, 1)
        high = from_behind(lax.slice_in_dim(block, 0, 1, axis=dim), axis, -1)
        block = jnp.concatenate([low, block, high], axis=dim)
    return block


def fold_halo(block):
    for axis, dim in (("gx", 0), ("gy", 1)):
        size = block.shape[dim]
        high = from_behind(lax.slice_in_dim(block, 0, 1, axis=dim).astype(BF), axis, -1).astype(F32)
        low = from_behind(lax.slice_in_dim(block, size - 1, size, axis=dim).astype(BF), axis, 1).astype(F32)
        inner = lax.slice_in_dim(block, 1, size - 1, axis=dim)
        first = lax.slice_in_dim(inner, 0, 1, axis=dim) + low
        last = lax.slice_in_dim(inner, size - 3, size - 2, axis=dim) + high
        block = jnp.concatenate([first, lax.slice_in_dim(inner, 1, size - 3, axis=dim), last], axis=dim)
    return block


def total_over_devices(rows):
    axes = ("gx", "gy")
    count = lax.axis_size("gx") * lax.axis_size("gy")
    parts = lax.all_to_all(rows.reshape(count, -1, L), axes, 0, 0)
    mine = jnp.sum(parts.astype(F32), axis=0).astype(BF)
    spread = jnp.broadcast_to(mine[None], (count,) + mine.shape)
    return lax.all_to_all(spread, axes, 0, 0).reshape(-1, L)


def on_device(
    latent, offset, owner, slot, cotangent, edge_in, edge_geo, edge_mid, edge_out, node_in, node_out, biases, ln_gain
):
    cells_x, cells_y, cap_size, width_l = cotangent.shape
    slots = cells_x * cells_y * cap_size
    width = cells_y + 2
    halo_rows = (cells_x + 2) * width * cap_size
    count_x = lax.axis_size("gx")
    count_y = lax.axis_size("gy")
    my_x = lax.axis_index("gx")
    my_y = lax.axis_index("gy")
    rows = latent.shape[0]
    send = rows // 9
    step_x = (owner // count_y - my_x + 1) % count_x
    step_y = (owner % count_y - my_y + 1) % count_y
    bucket = (step_x * 3 + step_y)[None, :]
    mark = slot + 1
    ones = jnp.ones((rows,), F32)
    zeros = jnp.zeros((rows,), F32)
    meta = jnp.stack(
        [
            offset[0].astype(F32), offset[1].astype(F32), ones, (mark // 16).astype(F32), (mark % 16).astype(F32),
            zeros, zeros, zeros,
        ]
    )
    (sent,) = call(sort_kernel, [((rows, 2 * L), BF)], [], latent, bucket, meta)
    sent = sent.reshape(3, 3, send, 2 * L)
    sections = [sent[:, 1], from_behind(sent[:, 2], "gy", 1), from_behind(sent[:, 0], "gy", -1)]
    section = jnp.stack(sections)
    final = [section[:, 1], from_behind(section[:, 2], "gx", 1), from_behind(section[:, 0], "gx", -1)]
    arrived = jnp.concatenate([piece.reshape(-1, 2 * L) for piece in final], axis=0)
    (pay,) = call(place_kernel, [((slots, 2 * L), BF)], [], arrived)
    halo = with_halo(pay.reshape(cells_x, cells_y, cap_size, 2 * L)).reshape(halo_rows, 2 * L)
    weights = (edge_in, edge_geo, edge_mid, edge_out, node_in, node_out, biases, ln_gain)
    node = ((slots, L), F32)
    node_low = ((slots, L), BF)
    geometry = [((EDGES, 2 * L), BF), ((EDGES, L), BF), ((L, EDGES), F32), ((L, EDGES), F32), ((80, EDGES), BF)]
    wide = ((2 * L, 2 * L), BF)
    edge_scratch = [((halo_rows, L), F32), node, node]
    firsts = call(
        functools.partial(first_kernel, width),
        geometry + [node_low, node, node_low, node_low, node, node_low, node, node],
        edge_scratch + [wide],
        halo, pay, *weights,
        mib=20,
    )
    lhs, weight, weight_t, radius_t, hot_t, v1, wsum0 = firsts[:7]
    saved0 = firsts[7:]
    v1_halo = with_halo(v1.reshape(cells_x, cells_y, cap_size, L)).reshape(halo_rows, L)
    edge_outs = [node, ((halo_rows, L), F32), node, ((GROWS, L), BF)]
    edge_scratch += [((2 * L, 2 * L), F32), ((96, 2 * L), F32), ((8, 2 * L), F32), wide, wide, ((8, L), F32)]
    kept = ((slots // (2 * CAP) * EDGES, 2 * L), BF)
    v2, d_own1, d_far1, grad1, grads1 = call(
        functools.partial(middle_kernel, width),
        [node_low] + edge_outs,
        edge_scratch + [node, kept, kept, kept],
        v1_halo, halo, pay, v1, cotangent.reshape(slots, L), lhs, weight, weight_t, radius_t, hot_t, *weights,
        mib=44,
    )
    d_far1 = fold_halo(d_far1.reshape(cells_x + 2, width, cap_size, L)).reshape(slots, L)
    d_own0, d_far0, grad0, grads0 = call(
        functools.partial(back_kernel, width),
        edge_outs,
        edge_scratch,
        d_own1, d_far1, grad1, halo, pay, lhs, weight, radius_t, hot_t, wsum0, *saved0, *weights,
        mib=20,
    )
    d_far0 = fold_halo(d_far0.reshape(cells_x + 2, width, cap_size, L)).reshape(slots, L)
    (latent_grad,) = call(last_kernel, [node], [], d_own0, d_far0, grad0, edge_in, pay)
    total = total_over_devices(jnp.concatenate([grads0, grads1], axis=0))
    scale = float(slots * count_x * count_y) ** -0.5
    grads = call(
        functools.partial(unpack_kernel, scale),
        [
            ((STEPS, L, 2 * L), F32), ((STEPS, 3, L), F32), ((STEPS, L, L), F32), ((STEPS, L, L), F32),
            ((STEPS, 2 * L, L), F32), ((STEPS, L, L), F32), ((STEPS, 5, L), F32), ((STEPS, L), F32),
        ],
        [],
        total,
    )
    cells = (cells_x, cells_y, cap_size, width_l)
    return (v2.reshape(cells), latent_grad.reshape(cells), *grads)


def solution(mesh):
    rows = P(("gx", "gy"))
    grid = P("gx", "gy", None, None)
    in_specs = (P(("gx", "gy"), None), P(None, ("gx", "gy")), rows, rows, grid) + (P(),) * 8
    out_specs = (grid, grid) + (P(),) * 8
    return jax.shard_map(on_device, mesh=mesh, in_specs=in_specs, out_specs=out_specs, check_vma=False)
```

```python
import functools

import jax
import jax.numpy as jnp
from jax import lax
from jax.experimental import pallas as pl
from jax.experimental.pallas import tpu as pltpu
from jax.sharding import PartitionSpec as P

STEPS = 2
LN_EPS = 1e-05
F32 = jnp.float32
BF = jnp.bfloat16
L = 128
CAP = 8
NEAR = 9 * CAP
EDGES = CAP * NEAR
GROWS = 1024


def dot(a, b):
    return jnp.dot(a, b, preferred_element_type=F32)


def dot_tn(a, b):
    return lax.dot_general(a, b, (((0,), (0,)), ((), ())), preferred_element_type=F32)


def dot_nt(a, b):
    return lax.dot_general(a, b, (((1,), (1,)), ((), ())), preferred_element_type=F32)


def iota(shape, dim):
    return lax.broadcasted_iota(jnp.int32, shape, dim)


def mask(cond):
    return jnp.where(cond, 1.0, 0.0).astype(F32)


def slope_of(half, tanh_half):
    sig = 0.5 + 0.5 * tanh_half
    act = half + half * tanh_half
    return sig + act * (1.0 - sig)


def wrapped_step(target, mine, count):
    step = target - mine.astype(F32) + 1.0
    step = jnp.where(step < 0.0, step + count, step)
    return jnp.where(step >= count, step - count, step)


def sort_kernel(count_x, count_y, latent_ref, offset_ref, owner_ref, slot_ref, out_ref):
    rows = latent_ref.shape[0]
    send = rows // 9
    owner = owner_ref[...].astype(F32)
    owner_x = jnp.floor((owner + 0.5) * (1.0 / count_y))
    owner_y = owner - owner_x * count_y
    bucket = 3.0 * wrapped_step(owner_x, lax.axis_index("gx"), count_x)
    bucket = bucket + wrapped_step(owner_y, lax.axis_index("gy"), count_y)
    hot = mask(iota((16, rows), 0).astype(F32) == bucket)
    upper = mask(iota((rows, rows), 0) <= iota((rows, rows), 1)).astype(BF)
    count = dot(hot.astype(BF), upper)
    rank = jnp.sum(hot * (count - 1.0), axis=0, keepdims=True)
    target = bucket * float(send) + rank
    perm = mask(iota((rows, rows), 0).astype(F32) == target).astype(BF)
    out_ref[:, :L] = dot(perm, latent_ref[...]).astype(BF)
    mark = (slot_ref[...] + 1).astype(F32)
    high = jnp.floor(mark * (1.0 / 16.0))
    meta = [offset_ref[...].astype(F32), jnp.ones_like(mark), high, mark - 16.0 * high, jnp.zeros((L - 5, rows), F32)]
    out_ref[:, L:] = dot_nt(perm, jnp.concatenate(meta, axis=0).astype(BF)).astype(BF)


def place_kernel(rows_ref, pay_ref):
    rows = rows_ref.shape[0]
    slots = pay_ref.shape[0]
    pick_lane = iota((8, L), 1)
    pick = jnp.where(pick_lane == 3, 16.0, jnp.where(pick_lane == 4, 1.0, 0.0)).astype(BF)
    mark = dot_nt(pick, rows_ref[:, L:])[0:1]
    hot = mask((iota((slots, rows), 0) + 1).astype(F32) == mark).astype(BF)
    pay_ref[...] = dot(hot, rows_ref[...]).astype(BF)


def fill_geometry(geo, width, lhs_ref, weight_ref, weight_t_ref, radius_t_ref, hot_t_ref):
    halo_rows = geo.shape[0]
    rows = dot_nt(mask(iota((8, L), 0) == iota((8, L), 1)).astype(BF), geo)
    cell = iota((halo_rows, L), 1) * CAP
    row = iota((halo_rows, L), 0)
    cell_hot = mask((row >= cell) & (row < cell + CAP)).astype(BF)
    slot_hot = mask((iota((8, halo_rows), 1) & (CAP - 1)) == iota((8, halo_rows), 0))
    px, py, occ = (dot((slot_hot * rows[k : k + 1]).astype(BF), cell_hot) for k in range(3))
    near = ([], [], [])
    for a in (-1, 0, 1):
        for b in (-1, 0, 1):
            shift = (-(width * a + b)) % L
            for piece, value, base in zip(near, (px, py, occ), (a, b, 0)):
                moved = value if shift == 0 else pltpu.roll(value, shift, 1)
                piece.append(moved + float(base))
    near_x, near_y, near_occ = (jnp.concatenate(piece, axis=0) for piece in near)
    radius, weight, hots = [], [], []
    lane = iota((NEAR, L), 1)
    sub = iota((NEAR, L), 0)
    for i in range(CAP):
        dx = near_x - px[i : i + 1]
        dy = near_y - py[i : i + 1]
        r2 = dx * dx + dy * dy
        reach = jnp.maximum(1.0 - r2, 0.0)
        w = occ[i : i + 1] * near_occ * reach * reach
        radius.append(r2)
        weight.append(jnp.where(sub == 4 * CAP + i, 0.0, w))
        hots.append(mask((sub == lane) | (lane == NEAR + i) | (lane == NEAR + CAP + i)))
    radius = jnp.concatenate(radius, axis=0)
    weight = jnp.concatenate(weight, axis=0)
    hots = jnp.concatenate(hots, axis=0)
    lhs_ref[:, :L] = hots.astype(BF)
    lhs_ref[:, L:] = radius.astype(BF)
    weight_ref[...] = weight.astype(BF)
    weight_t_ref[...] = weight.T
    radius_t_ref[...] = radius.T
    hot_t_ref[...] = hots.T[:80].astype(BF)


def column(value, k):
    return value[:, k : k + 1].astype(F32)


def fill_pre(far, geo_halo, own, geo_own, edge_geo, far_ref, near_ref):
    g0 = 0.5 * edge_geo[0:1].astype(F32)
    g1 = 0.5 * edge_geo[1:2].astype(F32)
    far_ref[...] = 0.5 * far.astype(F32) + column(geo_halo, 0) * g0 + column(geo_halo, 1) * g1
    near_ref[...] = 0.5 * own - column(geo_own, 0) * g0 - column(geo_own, 1) * g1


def shift_rows(edge_geo):
    g0 = 0.5 * edge_geo[0:1].astype(F32)
    g1 = 0.5 * edge_geo[1:2].astype(F32)
    side = iota((3 * CAP, L), 0) // CAP - 1
    return [float(a) * g0 + side.astype(F32) * g1 for a in (-1, 0, 1)]


def twice(row):
    return jnp.concatenate([row, row], axis=1)


def block_diag(w):
    zero = jnp.zeros_like(w)
    return jnp.concatenate(
        [jnp.concatenate([w, zero], axis=1), jnp.concatenate([zero, w], axis=1)], axis=0
    )


def pair_place(pair, cells_y):
    half = cells_y // 2
    x = pair // half
    y = (pair - x * half) * 2
    return x, y


def pair_rhs(pair, width, far_ref, near_ref, shifts, g2):
    x, y = pair_place(pair, width - 2)
    tops = []
    for k in range(2):
        pieces = []
        for a in range(3):
            start = pl.multiple_of(((x + a) * width + y + k) * CAP, CAP)
            pieces.append(far_ref[pl.ds(start, 3 * CAP), :] + shifts[a])
        mine = near_ref[pl.ds(pl.multiple_of((pair * 2 + k) * CAP, CAP), CAP), :]
        pieces.append(mine)
        pieces.append(mine - mine.astype(BF).astype(F32))
        pieces.append(jnp.zeros((L - NEAR - 2 * CAP, L), F32))
        tops.append(jnp.concatenate(pieces, axis=0))
    top = jnp.concatenate(tops, axis=1).astype(BF)
    hot = pair_hot(pair, width)
    return jnp.concatenate([top, jnp.where(hot, g2, 0.0).astype(BF)], axis=0)


def pair_hot(pair, width):
    x, y = pair_place(pair, width - 2)
    first = (x + 1) * width + y + 1
    lane = iota((L, 2 * L), 1)
    return iota((L, 2 * L), 0) == first + jnp.where(lane >= L, 1, 0)


def pair_rows(pair, width, ref):
    x, y = pair_place(pair, width - 2)
    first = (x + 1) * width + y + 1
    return ref[pl.ds(first, 1), :], ref[pl.ds(first + 1, 1), :]


def staggered(count, stages):
    state = [{} for _ in range(count)]
    for tick in range(count + len(stages) - 1):
        for depth in range(len(stages)):
            if 0 <= tick - depth < count:
                stages[depth](tick - depth, state[tick - depth])


def edges_forward(
    width, lhs_ref, weight_t_ref, far_ref, near_ref, shifts, g2, mid2_ref, bias2, sums_ref, wsum_ref, keep=None
):
    pairs = sums_ref.shape[0] // (2 * CAP)
    group = 8
    col = iota((CAP, EDGES), 1)
    start = iota((CAP, EDGES), 0) * NEAR
    own = mask((col >= start) & (col < start + NEAR))

    def body(step, carry):
        def first(k, s):
            pair = step * group + k
            rhs = pair_rhs(pair, width, far_ref, near_ref, shifts, g2)
            pre_one = dot(lhs_ref[...], rhs).astype(BF)
            tanh_one = jnp.tanh(pre_one)
            s["hidden"] = pre_one + pre_one * tanh_one
            if keep is not None:
                at = pl.ds(pl.multiple_of(pair * EDGES, EDGES), EDGES)
                keep[0][at, :] = s["hidden"]
                keep[1][at, :] = slope_of(pre_one, tanh_one)

        def second(k, s):
            pair = step * group + k
            pre_two = (dot(s["hidden"], mid2_ref[...]) + bias2).astype(BF)
            tanh_two = jnp.tanh(pre_two)
            s["act"] = pre_two + pre_two * tanh_two
            if keep is not None:
                at = pl.ds(pl.multiple_of(pair * EDGES, EDGES), EDGES)
                keep[2][at, :] = slope_of(pre_two, tanh_two)

        def third(k, s):
            pair = step * group + k
            row_a, row_b = pair_rows(pair, width, weight_t_ref)
            spread = jnp.concatenate([own * row_a, own * row_b], axis=0)
            sums = dot(spread.astype(BF), s["act"])
            at = pl.ds(pl.multiple_of(pair * 2 * CAP, 2 * CAP), 2 * CAP)
            sums_ref[at, :] = jnp.concatenate([sums[:CAP, :L], sums[CAP:, L:]], axis=0)
            wsum_ref[at, :] = jnp.broadcast_to(jnp.sum(spread, axis=1, keepdims=True), (2 * CAP, L))

        staggered(group, (first, second, third))
        return carry

    lax.fori_loop(0, pairs // group, body, 0)


def edges_backward(
    width, lhs_ref, weight_ref, radius_t_ref, hot_t_ref, far_ref, near_ref, shifts, g2, mid2_ref, mid2_t_ref, bias2,
    d_sums_ref, d_own_ref, d_far_ref, mid_ref, rows_ref, bias_ref, keep=None,
):
    pairs = d_own_ref.shape[0] // (2 * CAP)
    group = 8
    for ref in (d_far_ref, mid_ref, rows_ref, bias_ref):
        ref[...] = jnp.zeros_like(ref)

    def body(step, carry):
        def first(k, s):
            pair = step * group + k
            rhs = pair_rhs(pair, width, far_ref, near_ref, shifts, g2)
            pre_one = dot(lhs_ref[...], rhs).astype(BF)
            tanh_one = jnp.tanh(pre_one)
            s["hidden"] = pre_one + pre_one * tanh_one
            s["slope"] = slope_of(pre_one, tanh_one)

        def second(k, s):
            pair = step * group + k
            if keep is None:
                pre_two = (dot(s["hidden"], mid2_ref[...]) + bias2).astype(BF)
                slope_two = slope_of(pre_two, jnp.tanh(pre_two))
            else:
                at = pl.ds(pl.multiple_of(pair * EDGES, EDGES), EDGES)
                s["hidden"], s["slope"], slope_two = (ref[at, :] for ref in keep)
            pick = mask(pair_hot(pair, width)).astype(BF)
            weight = dot(weight_ref[...], pick)
            d_sums = d_sums_ref[pl.ds(pl.multiple_of(pair * 2 * CAP, 2 * CAP), 2 * CAP), :]
            d_sums = jnp.concatenate([d_sums[:CAP], d_sums[CAP:]], axis=1)
            d_sums = jnp.broadcast_to(d_sums[:, None, :], (CAP, NEAR, 2 * L)).reshape(EDGES, 2 * L)
            d_two = weight * d_sums * slope_two
            bias_ref[...] += jnp.sum(d_two.reshape(EDGES // 8, 8, 2 * L), axis=0)
            s["two"] = d_two.astype(BF)

        def third(k, s):
            mid_ref[...] += dot_tn(s["hidden"], s["two"])
            s["one"] = (dot(s["two"], mid2_t_ref[...]) * s["slope"]).astype(BF)

        def fourth(k, s):
            pair = step * group + k
            x, y = pair_place(pair, width - 2)
            rad_a, rad_b = pair_rows(pair, width, radius_t_ref)
            tail = jnp.concatenate([rad_a, rad_b, jnp.zeros((14, EDGES), F32)], axis=0).astype(BF)
            back = dot(jnp.concatenate([hot_t_ref[...], tail], axis=0), s["one"])
            rows_ref[...] += back
            own_rows = back[NEAR : NEAR + CAP]
            at = pl.ds(pl.multiple_of(pair * 2 * CAP, 2 * CAP), 2 * CAP)
            d_own_ref[at, :] = jnp.concatenate([own_rows[:, :L], own_rows[:, L:]], axis=0)
            for a in range(3):
                piece = back[3 * CAP * a : 3 * CAP * (a + 1)]
                zero = jnp.zeros((CAP, L), F32)
                both = jnp.concatenate([piece[:, :L], zero], axis=0) + jnp.concatenate([zero, piece[:, L:]], axis=0)
                at = pl.ds(pl.multiple_of(((x + a) * width + y) * CAP, CAP), 4 * CAP)
                d_far_ref[at, :] += both

        staggered(group, (second, third, fourth) if keep is not None else (first, second, third, fourth))
        return carry

    lax.fori_loop(0, pairs // group, body, 0)


def geo_grads(rows, d_far, geo_halo, d_own, geo_own):
    def total(value):
        return jnp.sum(value, axis=0, keepdims=True)

    rows = jnp.concatenate([rows[: NEAR, :L] + rows[: NEAR, L:], rows[80:82, :L], rows[80:82, L:]], axis=0)
    block = [total(rows[CAP * k : CAP * (k + 1)]) for k in range(9)]
    grad_x = sum(float(k // 3 - 1) * block[k] for k in range(9) if k // 3 != 1)
    grad_y = sum(float(k % 3 - 1) * block[k] for k in range(9) if k % 3 != 1)
    grad_x = grad_x + total(column(geo_halo, 0) * d_far) - total(column(geo_own, 0) * d_own)
    grad_y = grad_y + total(column(geo_halo, 1) * d_far) - total(column(geo_own, 1) * d_own)
    grad_r = rows[NEAR : NEAR + 1] + rows[NEAR + 3 : NEAR + 4]
    return grad_x, grad_y, grad_r


def node_forward(latent, occ, sums, wsum, w_out, w_first, w_second, biases, gain):
    bias = biases.astype(F32)
    sums_low = sums.astype(BF)
    message_low = (dot(sums_low, w_out) + wsum * bias[1:2]).astype(BF)
    first_pre = dot(latent, w_first[:L]) + dot(message_low, w_first[L:]) + bias[2:3]
    half = 0.5 * first_pre
    first_low = (half + half * jnp.tanh(half)).astype(BF)
    second = dot(first_low, w_second) + bias[3:4]
    centred = second - jnp.mean(second, axis=1, keepdims=True)
    inv_root = lax.rsqrt(jnp.mean(centred * centred, axis=1, keepdims=True) + LN_EPS)
    normed = centred * inv_root
    update = normed * gain.astype(F32) + bias[4:5]
    new = (latent.astype(F32) + occ * update).astype(BF)
    return new, (sums_low, message_low, half, first_low, normed, inv_root)


def node_backward(d_new, latent, occ, wsum, saved, w_out, w_first, w_second, gain):
    sums_low, message_low, half, first_low, normed, inv_root = saved

    def total(value):
        return jnp.sum(value, axis=0, keepdims=True)

    d_update = occ * d_new
    grad_gain = total(d_update * normed)
    grad_shift = total(d_update)
    d_normed = d_update * gain.astype(F32)
    d_second = inv_root * (
        d_normed
        - jnp.mean(d_normed, axis=1, keepdims=True)
        - normed * jnp.mean(d_normed * normed, axis=1, keepdims=True)
    )
    d_second_low = d_second.astype(BF)
    grad_second = dot_tn(first_low, d_second_low)
    d_first = dot_nt(d_second_low, w_second) * slope_of(half, jnp.tanh(half))
    d_first_low = d_first.astype(BF)
    grad_first = [dot_tn(latent, d_first_low), dot_tn(message_low, d_first_low)]
    d_latent = dot_nt(d_first_low, w_first[:L])
    d_message = dot_nt(d_first_low, w_first[L:])
    d_message_low = d_message.astype(BF)
    grad_out = dot_tn(sums_low, d_message_low)
    d_sums = dot_nt(d_message_low, w_out)
    small = [total(wsum * d_message), total(d_first), total(d_second), grad_shift, grad_gain]
    return d_sums, d_latent, grad_out, grad_first, grad_second, small


def store_node_grads(grads_ref, small_ref, grad_out, grad_first, grad_second, small):
    base = 3 * L
    for block in (grad_out, grad_first[0], grad_first[1], grad_second):
        grads_ref[base : base + L, :] = block.astype(BF)
        base += L
    small_ref[...] = jnp.concatenate(small + [jnp.zeros((3, L), F32)], axis=0)


def store_edge_grads(grads_ref, small_ref, latent, latent_halo, d_own, d_far, mid, bias, geo):
    grads_ref[:L, :] = dot_tn(latent, d_own.astype(BF)).astype(BF)
    grads_ref[L : 2 * L, :] = dot_tn(latent_halo, d_far.astype(BF)).astype(BF)
    grads_ref[2 * L : 3 * L, :] = (mid[:L, :L] + mid[L:, L:]).astype(BF)
    bias = jnp.sum(bias, axis=0, keepdims=True)
    rows = [bias[:, :L] + bias[:, L:], small_ref[:5, :]] + list(geo)
    grads_ref[7 * L :, :] = jnp.concatenate(rows + [jnp.zeros((L - 9, L), F32)], axis=0).astype(BF)


class Step:
    def __init__(self, refs, t):
        names = ("edge_in", "edge_geo", "edge_mid", "edge_out", "node_in", "node_out", "biases")
        for name, ref in zip(names, refs):
            setattr(self, name, ref[t])
        self.gain = refs[7][t : t + 1, :]


def prepare(w, latent_halo, geo_halo, latent, geo_own, far_ref, near_ref, mid2_ref, mid2_t_ref=None):
    far = dot(latent_halo, w.edge_in[:, L:]).astype(BF)
    own = dot(latent, w.edge_in[:, :L])
    fill_pre(far, geo_halo, own, geo_own, w.edge_geo, far_ref, near_ref)
    mid = w.edge_mid.astype(F32)
    mid2_ref[...] = block_diag(0.5 * mid).astype(BF)
    if mid2_t_ref is not None:
        mid2_t_ref[...] = block_diag(mid.T).astype(BF)
    bias2 = twice(0.5 * w.biases[0:1].astype(F32))
    g2 = twice(0.5 * w.edge_geo[2:3].astype(F32))
    return shift_rows(w.edge_geo), g2, bias2


def first_kernel(width, halo_ref, pay_ref, *refs):
    w = Step(refs[:8], 0)
    lhs_ref, weight_ref, weight_t_ref, radius_t_ref, hot_t_ref, new_ref, wsum_ref = refs[8:15]
    saved_refs = refs[15:20]
    inv_ref, far_ref, near_ref, sums_ref, mid2_ref = refs[20:]
    fill_geometry(halo_ref[:, L:], width, lhs_ref, weight_ref, weight_t_ref, radius_t_ref, hot_t_ref)
    latent, geo_own = pay_ref[:, :L], pay_ref[:, L:]
    shifts, g2, bias2 = prepare(
        w, halo_ref[:, :L], halo_ref[:, L:], latent, geo_own, far_ref, near_ref, mid2_ref
    )
    edges_forward(width, lhs_ref, weight_t_ref, far_ref, near_ref, shifts, g2, mid2_ref, bias2, sums_ref, wsum_ref)
    new, saved = node_forward(
        pay_ref[:, :L], column(pay_ref[:, L:], 2), sums_ref[...], wsum_ref[...], w.edge_out, w.node_in, w.node_out,
        w.biases, w.gain,
    )
    for ref, value in zip(saved_refs, saved):
        ref[...] = value
    inv_ref[...] = jnp.broadcast_to(saved[5], inv_ref.shape)
    new_ref[...] = new


def backward(
    width, w, d_new, latent_halo_ref, latent_ref, halo_ref, pay_ref, saved, wsum_ref, geometry, consts, outs, scratch, keep
):
    lhs_ref, weight_ref, radius_t_ref, hot_t_ref = geometry
    d_own_ref, d_far_ref, grad_ref, grads_ref = outs
    far_ref, near_ref, sums_ref, mid_ref, rows_ref, bias_ref, mid2_ref, mid2_t_ref, small_ref = scratch
    shifts, g2, bias2 = consts
    d_sums, d_latent, grad_out, grad_first, grad_second, small = node_backward(
        d_new, latent_ref[:, :L], column(pay_ref[:, L:], 2), wsum_ref[...], saved, w.edge_out, w.node_in, w.node_out,
        w.gain,
    )
    sums_ref[...] = d_sums
    grad_ref[...] = d_new + d_latent
    store_node_grads(grads_ref, small_ref, grad_out, grad_first, grad_second, small)
    edges_backward(
        width, lhs_ref, weight_ref, radius_t_ref, hot_t_ref, far_ref, near_ref, shifts, g2, mid2_ref, mid2_t_ref, bias2,
        sums_ref, d_own_ref, d_far_ref, mid_ref, rows_ref, bias_ref, keep,
    )
    geo = geo_grads(rows_ref[...], d_far_ref[...], halo_ref[:, L:], d_own_ref[...], pay_ref[:, L:])
    store_edge_grads(
        grads_ref, small_ref, latent_ref[:, :L], latent_halo_ref[:, :L], d_own_ref[...], d_far_ref[...], mid_ref[...],
        bias_ref[...], geo,
    )


def middle_kernel(width, latent_halo_ref, halo_ref, pay_ref, latent_ref, cot_ref, *refs):
    lhs_ref, weight_ref, weight_t_ref, radius_t_ref, hot_t_ref = refs[:5]
    w = Step(refs[5:13], 1)
    new_ref = refs[13]
    outs = refs[14:18]
    scratch = refs[18:27]
    wsum_ref = refs[27]
    keep = refs[28:]
    far_ref, near_ref, sums_ref = scratch[:3]
    mid2_ref, mid2_t_ref = scratch[6:8]
    consts = prepare(
        w, latent_halo_ref[...], halo_ref[:, L:], latent_ref[...], pay_ref[:, L:], far_ref, near_ref, mid2_ref, mid2_t_ref
    )
    shifts, g2, bias2 = consts
    edges_forward(
        width, lhs_ref, weight_t_ref, far_ref, near_ref, shifts, g2, mid2_ref, bias2, sums_ref, wsum_ref, keep
    )
    new, saved = node_forward(
        latent_ref[...], column(pay_ref[:, L:], 2), sums_ref[...], wsum_ref[...], w.edge_out, w.node_in, w.node_out,
        w.biases, w.gain,
    )
    new_ref[...] = new
    backward(
        width, w, cot_ref[...].astype(F32), latent_halo_ref, latent_ref, halo_ref, pay_ref, saved, wsum_ref,
        (lhs_ref, weight_ref, radius_t_ref, hot_t_ref), consts, outs, scratch, keep,
    )


def back_kernel(width, next_d_own_ref, next_d_far_ref, next_grad_ref, halo_ref, pay_ref, *refs):
    lhs_ref, weight_ref, radius_t_ref, hot_t_ref, wsum_ref = refs[:5]
    saved = tuple(ref[...] for ref in refs[5:11])
    w = Step(refs[11:19], 0)
    outs = refs[19:23]
    scratch = refs[23:]
    d_both = jnp.concatenate([next_d_own_ref[...], next_d_far_ref[...]], axis=1).astype(BF)
    d_new = next_grad_ref[...] + dot_nt(d_both, refs[11][1])
    consts = prepare(
        w, halo_ref[:, :L], halo_ref[:, L:], pay_ref[:, :L], pay_ref[:, L:], *scratch[:2], *scratch[6:8]
    )
    backward(
        width, w, d_new, halo_ref, pay_ref, halo_ref, pay_ref, saved, wsum_ref,
        (lhs_ref, weight_ref, radius_t_ref, hot_t_ref), consts, outs, scratch, None,
    )


def last_kernel(d_own_ref, d_far_ref, grad_ref, edge_in_ref, pay_ref, out_ref):
    d_both = jnp.concatenate([d_own_ref[...], d_far_ref[...]], axis=1).astype(BF)
    out_ref[...] = column(pay_ref[:, L:], 2) * (grad_ref[...] + dot_nt(d_both, edge_in_ref[0]))


def unpack_kernel(scale, rows_ref, in_ref, geo_ref, mid_ref, out_ref, first_ref, second_ref, bias_ref, gain_ref):
    gains = []
    for t in range(STEPS):
        def take(start, size, base=t * GROWS):
            return rows_ref[base + start : base + start + size, :].astype(F32) * scale

        in_ref[t, :, :L] = take(0, L)
        in_ref[t, :, L:] = take(L, L)
        mid_ref[t] = take(2 * L, L)
        out_ref[t] = take(3 * L, L)
        first_ref[t] = take(4 * L, 2 * L)
        second_ref[t] = take(6 * L, L)
        small = take(7 * L, 16)
        bias_ref[t] = small[:5]
        geo_ref[t] = small[6:9]
        gains.append(small[5:6])
    gain_ref[...] = jnp.concatenate(gains, axis=0)


def call(kernel, outs, scratch, *args, mib=8):
    return pl.pallas_call(
        kernel,
        out_shape=[jax.ShapeDtypeStruct(shape, dtype) for shape, dtype in outs],
        in_specs=[pl.BlockSpec(memory_space=pltpu.VMEM)] * len(args),
        out_specs=[pl.BlockSpec(memory_space=pltpu.VMEM)] * len(outs),
        scratch_shapes=[pltpu.VMEM(shape, dtype) for shape, dtype in scratch],
        compiler_params=pltpu.CompilerParams(vmem_limit_bytes=mib * 1024 * 1024),
    )(*args)


def from_behind(value, axis, steps):
    count = lax.axis_size(axis)
    return lax.ppermute(value, axis, [(source, (source + steps) % count) for source in range(count)])


def with_halo(block):
    for axis, dim in (("gx", 0), ("gy", 1)):
        size = block.shape[dim]
        low = from_behind(lax.slice_in_dim(block, size - 1, size, axis=dim), axis, 1)
        high = from_behind(lax.slice_in_dim(block, 0, 1, axis=dim), axis, -1)
        block = jnp.concatenate([low, block, high], axis=dim)
    return block


def fold_halo(block):
    for axis, dim in (("gx", 0), ("gy", 1)):
        size = block.shape[dim]
        high = from_behind(lax.slice_in_dim(block, 0, 1, axis=dim).astype(BF), axis, -1).astype(F32)
        low = from_behind(lax.slice_in_dim(block, size - 1, size, axis=dim).astype(BF), axis, 1).astype(F32)
        inner = lax.slice_in_dim(block, 1, size - 1, axis=dim)
        first = lax.slice_in_dim(inner, 0, 1, axis=dim) + low
        last = lax.slice_in_dim(inner, size - 3, size - 2, axis=dim) + high
        block = jnp.concatenate([first, lax.slice_in_dim(inner, 1, size - 3, axis=dim), last], axis=dim)
    return block


def total_over_devices(rows):
    axes = ("gx", "gy")
    count = lax.axis_size("gx") * lax.axis_size("gy")
    parts = lax.all_to_all(rows.reshape(count, -1, L), axes, 0, 0)
    mine = jnp.sum(parts.astype(F32), axis=0).astype(BF)
    spread = jnp.broadcast_to(mine[None], (count,) + mine.shape)
    return lax.all_to_all(spread, axes, 0, 0).reshape(-1, L)


def on_device(
    latent, offset, owner, slot, cotangent, edge_in, edge_geo, edge_mid, edge_out, node_in, node_out, biases, ln_gain
):
    cells_x, cells_y, cap_size, width_l = cotangent.shape
    slots = cells_x * cells_y * cap_size
    width = cells_y + 2
    halo_rows = (cells_x + 2) * width * cap_size
    count_x = lax.axis_size("gx")
    count_y = lax.axis_size("gy")
    rows = latent.shape[0]
    send = rows // 9
    (sent,) = call(
        functools.partial(sort_kernel, count_x, count_y), [((rows, 2 * L), BF)], [],
        latent, offset, owner[None, :], slot[None, :],
    )
    sent = sent.reshape(3, 3, send, 2 * L)
    sections = [sent[:, 1], from_behind(sent[:, 2], "gy", 1), from_behind(sent[:, 0], "gy", -1)]
    section = jnp.stack(sections)
    final = [section[:, 1], from_behind(section[:, 2], "gx", 1), from_behind(section[:, 0], "gx", -1)]
    arrived = jnp.concatenate([piece.reshape(-1, 2 * L) for piece in final], axis=0)
    (pay,) = call(place_kernel, [((slots, 2 * L), BF)], [], arrived)
    halo = with_halo(pay.reshape(cells_x, cells_y, cap_size, 2 * L)).reshape(halo_rows, 2 * L)
    weights = (edge_in, edge_geo, edge_mid, edge_out, node_in, node_out, biases, ln_gain)
    node = ((slots, L), F32)
    node_low = ((slots, L), BF)
    geometry = [((EDGES, 2 * L), BF), ((EDGES, L), BF), ((L, EDGES), F32), ((L, EDGES), F32), ((80, EDGES), BF)]
    wide = ((2 * L, 2 * L), BF)
    edge_scratch = [((halo_rows, L), F32), node, node]
    firsts = call(
        functools.partial(first_kernel, width),
        geometry + [node_low, node, node_low, node_low, node, node_low, node, node],
        edge_scratch + [wide],
        halo, pay, *weights,
        mib=20,
    )
    lhs, weight, weight_t, radius_t, hot_t, v1, wsum0 = firsts[:7]
    saved0 = firsts[7:]
    v1_halo = with_halo(v1.reshape(cells_x, cells_y, cap_size, L)).reshape(halo_rows, L)
    edge_outs = [node, ((halo_rows, L), F32), node, ((GROWS, L), BF)]
    edge_scratch += [((2 * L, 2 * L), F32), ((96, 2 * L), F32), ((8, 2 * L), F32), wide, wide, ((8, L), F32)]
    kept = ((slots // (2 * CAP) * EDGES, 2 * L), BF)
    v2, d_own1, d_far1, grad1, grads1 = call(
        functools.partial(middle_kernel, width),
        [node_low] + edge_outs,
        edge_scratch + [node, kept, kept, kept],
        v1_halo, halo, pay, v1, cotangent.reshape(slots, L), lhs, weight, weight_t, radius_t, hot_t, *weights,
        mib=44,
    )
    d_far1 = fold_halo(d_far1.reshape(cells_x + 2, width, cap_size, L)).reshape(slots, L)
    d_own0, d_far0, grad0, grads0 = call(
        functools.partial(back_kernel, width),
        edge_outs,
        edge_scratch,
        d_own1, d_far1, grad1, halo, pay, lhs, weight, radius_t, hot_t, wsum0, *saved0, *weights,
        mib=20,
    )
    d_far0 = fold_halo(d_far0.reshape(cells_x + 2, width, cap_size, L)).reshape(slots, L)
    (latent_grad,) = call(last_kernel, [node], [], d_own0, d_far0, grad0, edge_in, pay)
    total = total_over_devices(jnp.concatenate([grads0, grads1], axis=0))
    scale = float(slots * count_x * count_y) ** -0.5
    grads = call(
        functools.partial(unpack_kernel, scale),
        [
            ((STEPS, L, 2 * L), F32), ((STEPS, 3, L), F32), ((STEPS, L, L), F32), ((STEPS, L, L), F32),
            ((STEPS, 2 * L, L), F32), ((STEPS, L, L), F32), ((STEPS, 5, L), F32), ((STEPS, L), F32),
        ],
        [],
        total,
    )
    cells = (cells_x, cells_y, cap_size, width_l)
    return (v2.reshape(cells), latent_grad.reshape(cells), *grads)


def solution(mesh):
    rows = P(("gx", "gy"))
    grid = P("gx", "gy", None, None)
    in_specs = (P(("gx", "gy"), None), P(None, ("gx", "gy")), rows, rows, grid) + (P(),) * 8
    out_specs = (grid, grid) + (P(),) * 8
    return jax.shard_map(on_device, mesh=mesh, in_specs=in_specs, out_specs=out_specs, check_vma=False)
```
